32 devices in a mesh: expert: 8 (over z, y), wshard: 4 (over x, core).
Axes of the slice: x: 2, y: 2, z: 4, core: 2. Of those that a mesh axis runs over, the one named last changes fastest.
Arguments:
- tokens: bfloat16 [4096, 768], P(('expert', 'wshard')), may hold values from -6 to 6
- gain_attention: bfloat16 [768], P('wshard'), may hold values from 0.5 to 1.5
- gain_experts: bfloat16 [768], P('wshard'), may hold values from 0.5 to 1.5
- proj_inputs: bfloat16 [768, 2304], P('wshard'), may hold values from -0.21875 to 0.21875
- proj_output: bfloat16 [768, 768], P('wshard'), may hold values from -0.75 to 0.75
- bias_table: bfloat16 [32, 12], P('wshard'), may hold values from -4 to 4
- router_weight: bfloat16 [768, 16], P('wshard'), may hold values from -1 to 1
- routes: int32 [4096, 2], P(('expert', 'wshard')), may hold values from 0 to 15, as said below
- slot_index: int32 [4096, 2], P(('expert', 'wshard')), may hold values from 0 to 3, as said below
- drop_flags: int32 [4096, 2], P(('expert', 'wshard')), may hold values from 0 to 1, as said below
- expert_in: bfloat16 [16, 768, 3072], P('expert', None, 'wshard'), may hold values from -0.21875 to 0.21875
- expert_out: bfloat16 [16, 3072, 768], P('expert', 'wshard'), may hold values from -0.109375 to 0.109375
- cotangent: bfloat16 [4096, 768], P(('expert', 'wshard')), may hold values from -6 to 6
Outputs:
- output: bfloat16 [4096, 768], P(('expert', 'wshard'))
- grad_tokens: float32 [4096, 768], P(('expert', 'wshard'))
- grad_gain_attention: float32 [768], P('wshard')
- grad_gain_experts: float32 [768], P('wshard')
- grad_proj_inputs: float32 [768, 2304], P('wshard')
- grad_proj_output: float32 [768, 768], P('wshard')
- grad_bias_table: float32 [32, 12], P('wshard')
- grad_router: float32 [768, 16], P('wshard')
- grad_expert_in: float32 [16, 768, 3072], P('expert', None, 'wshard')
- grad_expert_out: float32 [16, 3072, 768], P('expert', 'wshard')
The draws below stay inside these ranges and needn't reach their ends.
Inputs may be any that keep to these rules, and one draw needn't show every extreme that they name: `routes`: each row names two different experts; one expert, drawn from the seed and the same for all devices, is the first choice of at least 8 of the rows of every device. `slot_index`: within the rows of one device and one expert, the kept entries take slots 0, 1, 2, ... once each in order of rows, all first choices before all second choices; an entry with drop flag 1 has slot 0; some expert has all 4 slots kept on every device. `drop_flags`: 1 exactly where an entry's rank among the entries of its device and expert, counted as for the slots, is 4 or more; every device drops some entries.
All inputs are finite; a program needn't handle non-finite values.
Results may differ from the reference program's by a relative error of at most 0.012.
The reference program's roundings to bfloat16 on the way count: a program that leaves them out, or rounds other values in their place, can miss the bound.
Values may be sent and summed in bfloat16 or wider, within the bound.
No kernel may reach another device: no remote copies, remote signals or barrier semaphores. Data moves between devices by JAX's collectives and lax.ppermute only.
A program may use at most 128 MiB of HBM per device.

```python
import math
import jax
import jax.numpy as jnp
from jax import lax

D = 768
H = 12
HD = 64
FF = 3072
NB = 32
MAXDIST = 128
TOK_DEV = 128
CAP = 4
EXPERTS = 16
LENGTH = 512
TOKENS = 4096


def permute_block(block_key):
    return jax.random.permutation(block_key, TOK_DEV)


def route_table(key):
    subkeys = jax.random.split(jax.random.fold_in(key, 1234), 7)
    popular = jax.random.permutation(subkeys[0], EXPERTS)
    draw_one = jax.random.randint(subkeys[1], (TOKENS,), 0, EXPERTS)
    draw_two = jax.random.randint(subkeys[2], (TOKENS,), 0, EXPERTS)
    draw_three = jax.random.randint(subkeys[3], (TOKENS,), 0, EXPERTS)
    first_expert = popular[jnp.minimum(jnp.minimum(draw_one, draw_two), draw_three)]
    favoured = jax.random.randint(subkeys[4], (), 0, EXPERTS)
    blocks = TOKENS // TOK_DEV
    positions = jax.vmap(permute_block)(jax.random.split(subkeys[5], blocks)).reshape(TOKENS)
    first_expert = jnp.where(positions < CAP + 4, favoured, first_expert)
    second = (first_expert + 1 + jax.random.randint(subkeys[6], (TOKENS,), 0, EXPERTS - 1)) % EXPERTS
    chosen = jnp.stack([first_expert, second], axis=1).astype(jnp.int32)
    onehot = (chosen.reshape(blocks, TOK_DEV, 2)[..., None] == jnp.arange(EXPERTS)).astype(jnp.int32)
    first_onehot = onehot[:, :, 0]
    second_onehot = onehot[:, :, 1]
    before_first = jnp.cumsum(first_onehot, axis=1) - first_onehot
    before_second = jnp.cumsum(second_onehot, axis=1) - second_onehot + jnp.sum(first_onehot, axis=1, keepdims=True)
    rank_first = jnp.sum(before_first * first_onehot, axis=-1)
    rank_second = jnp.sum(before_second * second_onehot, axis=-1)
    ranks_all = jnp.stack([rank_first, rank_second], axis=-1).reshape(TOKENS, 2)
    dropped = (ranks_all >= CAP).astype(jnp.int32)
    slots_all = jnp.where(dropped == 1, 0, ranks_all).astype(jnp.int32)
    return (chosen, slots_all, dropped)


def draw_routes(key, part):
    return route_table(key)[0]


def draw_slot_index(key, part):
    return route_table(key)[1]


def draw_drop_flags(key, part):
    return route_table(key)[2]


def draw_bias_table(key, part):
    subkeys = jax.random.split(jax.random.fold_in(key, 55), 1)
    table = jnp.clip(jax.random.normal(subkeys[0], (NB, H), jnp.float32), -4.0, 4.0)
    return table.astype(jnp.bfloat16)


def draw_router_weight(key, part):
    subkeys = jax.random.split(jax.random.fold_in(key, 77), 1)
    weights = jnp.clip(jax.random.normal(subkeys[0], (D, EXPERTS), jnp.float32), -5.0, 5.0) * (1.5 / D ** 0.5)
    return weights.astype(jnp.bfloat16)


def shard_levels(key, extent, cuts, low, largest):
    def one(dim, shards_of):
        steps = jax.random.uniform(jax.random.fold_in(jax.random.fold_in(key, 6), dim), (shards_of,), jnp.float32, low / len(cuts), largest / len(cuts))
        return jnp.repeat(jnp.exp(steps), extent[dim] // shards_of).reshape((-1,) + (1,) * (len(extent) - dim - 1))

    level = one(*cuts[0])
    for cut in cuts[1:]:
        level = level * one(*cut)
    return level


def scatter_about(key, dims, deviation, most, cuts=(), held_as=jnp.bfloat16):
    values = jax.random.normal(key, dims, jnp.float32) * deviation
    if len(cuts) > 0:
        values = shard_levels(key, dims, cuts, -0.22, 0.18) * values
    return jnp.clip(values, min=-most, max=most).astype(held_as)


def setup_inputs(seed: int = 0) -> dict:
    key_list = jax.random.split(jax.random.key(seed), 14)
    return {
        "tokens": scatter_about(key_list[0], (TOKENS, D), 1.0, 6.0, ((0, 32),)),
        "gain_attention": jnp.clip(1.0 + 0.1 * jax.random.normal(key_list[1], (D,), jnp.float32), 0.5, 1.5).astype(jnp.bfloat16),
        "gain_experts": jnp.clip(1.0 + 0.1 * jax.random.normal(key_list[2], (D,), jnp.float32), 0.5, 1.5).astype(jnp.bfloat16),
        "proj_inputs": scatter_about(key_list[3], (D, 3 * D), D ** -0.5, 0.21875, ((0, 4),)),
        "proj_output": scatter_about(key_list[4], (D, D), HD ** -0.5, 0.75, ((0, 4),)),
        "bias_table": draw_bias_table(jax.random.fold_in(key_list[13], 71), 0),
        "router_weight": draw_router_weight(jax.random.fold_in(key_list[13], 71), 0),
        "routes": draw_routes(jax.random.fold_in(key_list[13], 71), 0),
        "slot_index": draw_slot_index(jax.random.fold_in(key_list[13], 71), 0),
        "drop_flags": draw_drop_flags(jax.random.fold_in(key_list[13], 71), 0),
        "expert_in": scatter_about(key_list[10], (EXPERTS, D, FF), D ** -0.5, 0.21875, ((0, 8), (2, 4))),
        "expert_out": scatter_about(key_list[11], (EXPERTS, FF, D), FF ** -0.5, 0.109375, ((0, 8), (1, 4))),
        "cotangent": scatter_about(key_list[12], (TOKENS, D), 1.0, 6.0, ((0, 32),)),
    }


EPSILON = 1e-06
NEGATIVE = -1e+30

def distance_bucket(distance):
    exact_span = NB // 2
    bucket = jnp.zeros_like(distance) + exact_span
    for level in range(1, exact_span):
        threshold = math.ceil(exact_span * (MAXDIST / exact_span) ** (level / exact_span) - 1e-09)
        bucket = bucket + (distance >= threshold).astype(jnp.int32)
    return jnp.where(distance < exact_span, distance, bucket).astype(jnp.int32)

def norm_scale(values):
    return lax.rsqrt(lax.optimization_barrier(jnp.mean(values * values, axis=-1, keepdims=True)) + EPSILON)

def norm_backward(upstream, inputs, scale, gain):
    scaled = upstream * gain
    inner = lax.optimization_barrier(jnp.mean(scaled * inputs, axis=-1, keepdims=True))
    return scale * scaled - inputs * scale * scale * scale * inner

def rounded(values):
    return lax.optimization_barrier(values.astype(jnp.bfloat16)).astype(jnp.float32)

def sequence_scores(query_rows, key_rows, bucket_rows, table):
    scores = jnp.einsum('qhd,khd->hqk', query_rows, key_rows) * HD ** (-0.5)
    scores = scores + jnp.transpose(table[bucket_rows], (2, 0, 1))
    positions = jnp.arange(LENGTH)
    causal = positions[None, :] <= positions[:, None]
    return (jnp.where(causal[None], scores, NEGATIVE), causal)

def scatter_rows(first_rows, second_rows, flat, rows_total):
    buffer = jnp.zeros((rows_total, D), jnp.float32)
    buffer = buffer.at[flat[:, 0]].add(first_rows)
    buffer = buffer.at[flat[:, 1]].add(second_rows)
    return buffer.astype(jnp.bfloat16)

def reference(tokens, gain_attention, gain_experts, proj_inputs, proj_output, bias_table, router_weight, routes, slot_index, drop_flags, expert_in, expert_out, cotangent):
    inputs = tokens.astype(jnp.float32)
    gain_one = gain_attention.astype(jnp.float32)
    gain_two = gain_experts.astype(jnp.float32)
    scale_one = norm_scale(inputs)
    normed_one = (inputs * scale_one * gain_one).astype(jnp.bfloat16)
    projected = jnp.dot(normed_one, proj_inputs, preferred_element_type=jnp.float32).astype(jnp.bfloat16)
    sequences = TOKENS // LENGTH
    table = bias_table.astype(jnp.float32)
    heads_view = projected.astype(jnp.float32).reshape(sequences, LENGTH, 3, H, HD)
    seq_positions = jnp.arange(LENGTH, dtype=jnp.int32)
    distance = jnp.maximum(seq_positions[:, None] - seq_positions[None, :], 0).astype(jnp.int32)
    bucket_rows = distance_bucket(distance)

    def attend(block):
        scores, causal = sequence_scores(block[:, 0], block[:, 1], bucket_rows, table)
        row_max = lax.optimization_barrier(jnp.max(scores, axis=-1, keepdims=True))
        exponent = jnp.where(causal[None], jnp.exp(scores - row_max), 0.0)
        row_total = lax.optimization_barrier(jnp.sum(exponent, axis=-1, keepdims=True))
        weights = rounded(exponent / row_total)
        mixed_rows = jnp.einsum('hqk,khd->qhd', weights, block[:, 2])
        return (mixed_rows.reshape(LENGTH, D).astype(jnp.bfloat16), row_max + jnp.log(row_total))
    mixed, log_totals = lax.map(attend, heads_view)
    mixed = mixed.reshape(TOKENS, D)
    residual = inputs + jnp.dot(mixed, proj_output, preferred_element_type=jnp.float32)
    scale_two = norm_scale(residual)
    normed_two = (residual * scale_two * gain_two).astype(jnp.bfloat16)
    logits = jnp.dot(normed_two, router_weight, preferred_element_type=jnp.float32)
    chosen = jnp.take_along_axis(logits, routes, axis=1)
    chosen_max = lax.optimization_barrier(jnp.max(chosen, axis=1, keepdims=True))
    exponent = jnp.exp(chosen - chosen_max)
    gates = exponent / lax.optimization_barrier(jnp.sum(exponent, axis=1, keepdims=True))
    keep = (1 - drop_flags).astype(jnp.float32)
    used = gates * keep
    blocks = jnp.arange(TOKENS, dtype=jnp.int32) // TOK_DEV
    flat = ((blocks[:, None] * EXPERTS + routes) * CAP + slot_index).astype(jnp.int32)
    block_count = TOKENS // TOK_DEV
    rows_total = block_count * EXPERTS * CAP
    normed_float = normed_two.astype(jnp.float32)
    buffer = scatter_rows(normed_float * keep[:, 0:1], normed_float * keep[:, 1:2], flat, rows_total)
    upstream = cotangent.astype(jnp.float32)
    grad_buffer = scatter_rows(rounded(used[:, 0:1] * upstream), rounded(used[:, 1:2] * upstream), flat, rows_total)

    def expert_view(array):
        return jnp.transpose(array.reshape(block_count, EXPERTS, CAP, D), (1, 0, 2, 3)).reshape(EXPERTS, block_count * CAP, D)

    def flat_view(array):
        return jnp.transpose(array.reshape(EXPERTS, block_count, CAP, D), (1, 0, 2, 3)).reshape(rows_total, D)

    def expert_pass(packed):
        row_block, grad_block, weight_in, weight_out = packed
        pre_act = jnp.dot(row_block, weight_in, preferred_element_type=jnp.float32)
        hidden = jax.nn.gelu(pre_act).astype(jnp.bfloat16)
        result = jnp.dot(hidden, weight_out, preferred_element_type=jnp.float32).astype(jnp.bfloat16)
        grad_hidden = jnp.dot(grad_block, weight_out.T, preferred_element_type=jnp.float32)
        unused, pullback = jax.vjp(jax.nn.gelu, pre_act)
        grad_pre = pullback(grad_hidden)[0].astype(jnp.bfloat16)
        grad_in = jnp.dot(row_block.T, grad_pre, preferred_element_type=jnp.float32)
        grad_out = jnp.dot(hidden.T, grad_block, preferred_element_type=jnp.float32)
        grad_rows = jnp.dot(grad_pre, weight_in.T, preferred_element_type=jnp.float32).astype(jnp.bfloat16)
        return (result, grad_rows, grad_in, grad_out)
    results, grad_rows, grad_expert_in, grad_expert_out = lax.map(expert_pass, (expert_view(buffer), expert_view(grad_buffer), expert_in, expert_out))
    results = flat_view(results)
    grad_rows = flat_view(grad_rows)
    first_result = results[flat[:, 0]].astype(jnp.float32) * keep[:, 0:1]
    second_result = results[flat[:, 1]].astype(jnp.float32) * keep[:, 1:2]
    moe = used[:, 0:1] * first_result + used[:, 1:2] * second_result
    output = (residual + moe).astype(jnp.bfloat16)
    grad_gate = keep * jnp.stack([lax.optimization_barrier(jnp.sum(upstream * first_result, axis=1)), lax.optimization_barrier(jnp.sum(upstream * second_result, axis=1))], axis=1)
    mean_gate = lax.optimization_barrier(jnp.sum(gates * grad_gate, axis=1, keepdims=True))
    grad_chosen = gates * (grad_gate - mean_gate)
    expert_ids = jnp.arange(EXPERTS, dtype=jnp.int32)
    grad_logits = (routes[:, 0:1] == expert_ids).astype(jnp.float32) * grad_chosen[:, 0:1]
    grad_logits = grad_logits + (routes[:, 1:2] == expert_ids).astype(jnp.float32) * grad_chosen[:, 1:2]
    grad_logits_b = grad_logits.astype(jnp.bfloat16)
    grad_router = jnp.dot(normed_two.T, grad_logits_b, preferred_element_type=jnp.float32)
    grad_normed_two = jnp.dot(grad_logits_b, router_weight.T, preferred_element_type=jnp.float32)
    grad_normed_two = grad_normed_two + grad_rows[flat[:, 0]].astype(jnp.float32) * keep[:, 0:1]
    grad_normed_two = grad_normed_two + grad_rows[flat[:, 1]].astype(jnp.float32) * keep[:, 1:2]
    grad_gain_experts = lax.optimization_barrier(jnp.sum(grad_normed_two * residual * scale_two, axis=0))
    grad_residual = upstream + norm_backward(grad_normed_two, residual, scale_two, gain_two)
    grad_res_b = grad_residual.astype(jnp.bfloat16)
    grad_proj_output = jnp.dot(mixed.T, grad_res_b, preferred_element_type=jnp.float32)
    grad_mixed = jnp.dot(grad_res_b, proj_output.T, preferred_element_type=jnp.float32).astype(jnp.bfloat16)
    grad_view = grad_mixed.astype(jnp.float32).reshape(sequences, LENGTH, H, HD)

    def attend_back(packed):
        block, log_total, grad_block = packed
        scores, causal = sequence_scores(block[:, 0], block[:, 1], bucket_rows, table)
        weights = jnp.where(causal[None], jnp.exp(scores - log_total), 0.0)
        weights_b = rounded(weights)
        grad_value = jnp.einsum('hqk,qhd->khd', weights_b, grad_block)
        grad_weights = jnp.einsum('qhd,khd->hqk', grad_block, block[:, 2])
        inner = lax.optimization_barrier(jnp.sum(weights * grad_weights, axis=-1, keepdims=True))
        grad_scores = weights * (grad_weights - inner)
        grad_scores_b = rounded(grad_scores)
        grad_query = jnp.einsum('hqk,khd->qhd', grad_scores_b, block[:, 1]) * HD ** (-0.5)
        grad_key = jnp.einsum('hqk,qhd->khd', grad_scores_b, block[:, 0]) * HD ** (-0.5)
        grad_table = jax.ops.segment_sum(jnp.transpose(grad_scores, (1, 2, 0)).reshape(-1, H), bucket_rows.reshape(-1), num_segments=NB)
        stacked = jnp.stack([grad_query, grad_key, grad_value], axis=1).reshape(LENGTH, 3 * D)
        return (stacked.astype(jnp.bfloat16), grad_table)
    grad_projected, grad_tables = lax.map(attend_back, (heads_view, log_totals, grad_view))
    grad_projected = grad_projected.reshape(TOKENS, 3 * D)
    grad_bias_table = lax.optimization_barrier(jnp.sum(grad_tables, axis=0))
    grad_proj_inputs = jnp.dot(normed_one.T, grad_projected, preferred_element_type=jnp.float32)
    grad_normed_one = jnp.dot(grad_projected, proj_inputs.T, preferred_element_type=jnp.float32)
    grad_gain_attention = lax.optimization_barrier(jnp.sum(grad_normed_one * inputs * scale_one, axis=0))
    grad_tokens = grad_residual + norm_backward(grad_normed_one, inputs, scale_one, gain_one)
    return (output, grad_tokens, grad_gain_attention, grad_gain_experts, grad_proj_inputs, grad_proj_output, grad_bias_table, grad_router, grad_expert_in, grad_expert_out)
```

```python
import math

import jax
import jax.numpy as jnp
from jax import lax
from jax.experimental import pallas as pl
from jax.experimental.pallas import tpu as pltpu
from jax.sharding import PartitionSpec as P

NB = 32
MAXDIST = 128
CAP = 4
EPSILON = 1e-06
NEGATIVE = -1e30
BLOCK = 128
F32 = jnp.float32
BF16 = jnp.bfloat16


def bucket_starts():
    exact = NB // 2
    starts = list(range(exact + 1))
    for level in range(1, exact):
        starts.append(math.ceil(exact * (MAXDIST / exact) ** (level / exact) - 1e-09))
    return starts


STARTS = bucket_starts()


def exchange(value, axis, mask):
    size = lax.axis_size(axis)
    return lax.ppermute(value, axis, [(i, i ^ mask) for i in range(size)])


def gather_xor(value, axis):
    pieces = {0: value}
    bit = lax.axis_size(axis) // 2
    while bit >= 1:
        for key in list(pieces):
            pieces[key | bit] = exchange(pieces[key], axis, bit)
        bit //= 2
    return [pieces[k] for k in range(len(pieces))]


def whole(kernel, outs, *args, scratch=(), smem=1):
    specs = [pl.BlockSpec(memory_space=pltpu.SMEM)] * smem
    specs += [pl.BlockSpec(memory_space=pltpu.VMEM)] * (len(args) - smem)
    return pl.pallas_call(
        kernel,
        out_shape=[jax.ShapeDtypeStruct(s, d) for s, d in outs],
        in_specs=specs,
        out_specs=[pl.BlockSpec(memory_space=pltpu.VMEM)] * len(outs),
        scratch_shapes=list(scratch),
    )(*args)


def dot_nn(a, b):
    return lax.dot_general(a, b, (((1,), (0,)), ((), ())), preferred_element_type=F32)


def dot_nt(a, b):
    return lax.dot_general(a, b, (((1,), (1,)), ((), ())), preferred_element_type=F32)


def dot_tn(a, b):
    return lax.dot_general(a, b, (((0,), (0,)), ((), ())), preferred_element_type=F32)


def norm_scale(values):
    return lax.rsqrt(jnp.mean(values * values, axis=-1, keepdims=True) + EPSILON)


def sum_refs(refs):
    total = refs[0][...].astype(F32)
    for ref in refs[1:]:
        total = total + ref[...].astype(F32)
    return total


def distance_tile():
    rows = lax.broadcasted_iota(jnp.int32, (BLOCK, 2 * BLOCK), 0)
    cols = lax.broadcasted_iota(jnp.int32, (BLOCK, 2 * BLOCK), 1)
    return rows + BLOCK - cols


def rows_at(index, size):
    return pl.ds(pl.multiple_of(index * size, size & -size), size)


def prepare_kernel(groups, me_ref, w_ref, *outs_and_scratch):
    outs = outs_and_scratch[:groups]
    chunks = outs_and_scratch[groups]
    me = me_ref[0]
    third = w_ref.shape[1] // 3
    part = third // groups
    for d in range(groups):
        for s in range(3):
            chunks[d, :, s * part : (s + 1) * part] = w_ref[
                :, s * third + d * part : s * third + (d + 1) * part
            ]
    for k in range(groups):
        outs[k][...] = chunks[me ^ k]


def score_blocks(q, k, tile, far, qb, factor):
    blocks = []
    for kb in range(qb + 1):
        s = dot_nt(q, k[kb * BLOCK : (kb + 1) * BLOCK]) * factor
        if kb == qb:
            s = s + tile[:, BLOCK:]
        elif kb == qb - 1:
            s = s + tile[:, :BLOCK]
        else:
            s = s + far
        blocks.append(s)
    return blocks


def front_kernel(groups, heads, hs, me_ref, *refs):
    tok = refs[:groups]
    wp = refs[groups : 2 * groups]
    ext = refs[2 * groups : 3 * groups]
    outs = refs[3 * groups :]
    normed_ref, wfull_ref, proj_ref, mixed_ref, lse_ref, tile_ref, far_ref = outs[:7]
    pieces = outs[7 : 7 + groups]
    tab_ref = outs[7 + groups]
    me = me_ref[0]
    count = tok[0].shape[0]
    wrows = wp[0].shape[0]
    length = count * groups
    extra = sum_refs(ext)
    gain = extra[12:13, :]
    tab_ref[...] = extra
    for k in range(groups):
        x = tok[k][...].astype(F32)
        normed_ref[rows_at(me ^ k, count), :] = (x * norm_scale(x) * gain).astype(BF16)
        wfull_ref[rows_at(me ^ k, wrows), :] = wp[k][...]
    proj_ref[...] = dot_nn(normed_ref[...], wfull_ref[...]).astype(BF16)
    distance = distance_tile()
    factor = hs ** (-0.5)
    part = heads * hs
    lanes = lax.broadcasted_iota(jnp.int32, (BLOCK, 128), 1)
    for h in range(heads):
        row = tab_ref[pl.ds(me * heads + h, 1), :]
        tile = jnp.broadcast_to(row[:, 0:1], distance.shape)
        for n in range(1, NB):
            tile = jnp.where(distance >= STARTS[n], row[:, n : n + 1], tile)
        tile_ref[h] = jnp.where(distance >= 0, tile, NEGATIVE)
        far_ref[h] = jnp.broadcast_to(row[:, NB - 1 : NB], (8, 128))
    for qb in range(length // BLOCK):
        span = slice(qb * BLOCK, (qb + 1) * BLOCK)
        keys = (qb + 1) * BLOCK
        mixed = []
        lse = jnp.zeros((BLOCK, 128), F32)
        for h in range(heads):
            q = proj_ref[span, h * hs : (h + 1) * hs]
            k = proj_ref[:keys, part + h * hs : part + (h + 1) * hs]
            v = proj_ref[:keys, 2 * part + h * hs : 2 * part + (h + 1) * hs]
            blocks = score_blocks(q, k, tile_ref[h], far_ref[h, 0:1, 0:1], qb, factor)
            top = blocks[0]
            for s in blocks[1:]:
                top = jnp.maximum(top, s)
            top = jnp.max(top, axis=-1, keepdims=True)
            es = [jnp.exp(s - top) for s in blocks]
            total = es[0]
            for e in es[1:]:
                total = total + e
            total = jnp.sum(total, axis=-1, keepdims=True)
            inverse = 1.0 / total
            w = jnp.concatenate([(e * inverse).astype(BF16) for e in es], axis=1)
            mixed.append(dot_nn(w, v))
            lse = jnp.where(lanes == h, top + jnp.log(total), lse)
        mixed_ref[span, :] = jnp.concatenate(mixed, axis=1).astype(BF16)
        lse_ref[span, :] = lse
    for k in range(groups):
        pieces[k][...] = mixed_ref[rows_at(me ^ k, count), :]


def places_of(routes_ref, slot_ref, drop_ref, slots):
    count = routes_ref.shape[0]
    ids = lax.broadcasted_iota(jnp.int32, (count, slots), 1)
    flat = routes_ref[...] * CAP + slot_ref[...]
    flat = jnp.where(drop_ref[...] == 0, flat, -1)
    return [(flat[:, r : r + 1] == ids).astype(F32).astype(BF16) for r in range(2)]


def route_onehot(routes_ref, experts):
    count = routes_ref.shape[0]
    ids = lax.broadcasted_iota(jnp.int32, (count, experts), 1)
    routes = routes_ref[...]
    return [(routes[:, r : r + 1] == ids).astype(F32) for r in range(2)]


def middle_kernel(groups, experts, *refs):
    mixed = refs[:groups]
    wo = refs[groups : 2 * groups]
    ext = refs[2 * groups : 3 * groups]
    tok_ref, cot_ref, routes_ref, slot_ref, drop_ref = refs[3 * groups : 3 * groups + 5]
    residual_ref, normed_ref, send_ref, gates_ref = refs[3 * groups + 5 :]
    count, width = tok_ref.shape
    total = dot_nn(mixed[0][...], wo[0][...])
    for k in range(1, groups):
        total = total + dot_nn(mixed[k][...], wo[k][...])
    residual = tok_ref[...].astype(F32) + total
    residual_ref[...] = residual
    extra = sum_refs(ext)
    gain = extra[13:14, :]
    router = extra[16 : 16 + experts, :].astype(BF16)
    normed = (residual * norm_scale(residual) * gain).astype(BF16)
    normed_ref[...] = normed
    logits = dot_nt(normed, router)
    onehot = route_onehot(routes_ref, experts)
    chosen = [jnp.sum(logits * o, axis=1, keepdims=True) for o in onehot]
    top = jnp.maximum(chosen[0], chosen[1])
    ex = [jnp.exp(c - top) for c in chosen]
    both = ex[0] + ex[1]
    gates = [e / both for e in ex]
    keep = (1 - drop_ref[...]).astype(F32)
    places = places_of(routes_ref, slot_ref, drop_ref, experts * CAP)
    up = cot_ref[...].astype(F32)
    send_ref[:, :width] = dot_tn(places[0] + places[1], normed).astype(BF16)
    grads = dot_tn(places[0], (gates[0] * keep[:, 0:1] * up).astype(BF16))
    grads = grads + dot_tn(places[1], (gates[1] * keep[:, 1:2] * up).astype(BF16))
    send_ref[:, width:] = grads.astype(BF16)
    lanes = lax.broadcasted_iota(jnp.int32, (count, 128), 1)
    gates_ref[...] = jnp.where(lanes == 0, gates[0], gates[1])


def owner_mask(rows, local, j):
    index = lax.broadcasted_iota(jnp.int32, (rows, 1), 0)
    return (index // CAP) % local == j


def experts_kernel(groups, local, *refs):
    xs = refs[:groups]
    win_ref, wout_ref = refs[groups : groups + 2]
    hidden_ref, gpre_ref, send_ref, keep_ref, mid_ref, x_ref, acc_ref = refs[groups + 2 :]
    step = pl.program_id(0)
    rows = xs[0].shape[0]
    width = xs[0].shape[1] // 2

    @pl.when(step == 0)
    def _():
        for k in range(groups):
            x_ref[k * rows : (k + 1) * rows, :] = xs[k][...]
        acc_ref[...] = jnp.zeros_like(acc_ref)

    r = x_ref[:, :width]
    g = x_ref[:, width:]
    masks = [owner_mask(rows * groups, local, j) for j in range(local)]
    pre = dot_nn(r, win_ref[0])
    gh = dot_nt(g, wout_ref[0])
    for j in range(1, local):
        pre = jnp.where(masks[j], dot_nn(r, win_ref[j]), pre)
        gh = jnp.where(masks[j], dot_nt(g, wout_ref[j]), gh)
    root = math.sqrt(2.0 / math.pi)
    square = pre * pre
    th = jnp.tanh(root * (pre + 0.044715 * (square * pre)))
    cdf = 0.5 * (1.0 + th)
    hid = pre * cdf
    slope = cdf + 0.5 * pre * (1.0 - th * th) * (root * (1.0 + 3.0 * 0.044715 * square))
    gp = gh * slope
    hidden_ref[...] = hid.astype(BF16)
    gpre_ref[...] = gp.astype(BF16)
    for j in range(local):
        acc_ref[:, :width] += dot_nn(jnp.where(masks[j], hid, 0.0).astype(BF16), wout_ref[j])
        acc_ref[:, width:] += dot_nt(jnp.where(masks[j], gp, 0.0).astype(BF16), win_ref[j])

    @pl.when(step == pl.num_programs(0) - 1)
    def _():
        keep_ref[...] = acc_ref[0:rows, :]
        mid_ref[...] = acc_ref[2 * rows : 3 * rows, :]
        send_ref[0:rows, :] = acc_ref[rows : 2 * rows, :].astype(BF16)
        send_ref[rows : 2 * rows, :] = acc_ref[3 * rows : 4 * rows, :].astype(BF16)


def weights_kernel(groups, local, *refs):
    xs = refs[:groups]
    hidden_ref, gpre_ref, gin_ref, gout_ref, x_ref = refs[groups:]
    j = pl.program_id(0)
    rows = xs[0].shape[0]
    width = xs[0].shape[1] // 2

    @pl.when(pl.program_id(1) == 0)
    def _():
        for k in range(groups):
            x_ref[k * rows : (k + 1) * rows, :] = xs[k][...]

    mask = owner_mask(rows * groups, local, j)
    gp = jnp.where(mask, gpre_ref[...].astype(F32), 0.0).astype(BF16)
    hid = jnp.where(mask, hidden_ref[...].astype(F32), 0.0).astype(BF16)
    gin_ref[0] = dot_tn(x_ref[:, :width], gp)
    gout_ref[0] = dot_tn(hid, x_ref[:, width:])


def return_kernel(groups, experts, *refs):
    ext = refs[:groups]
    back_ref, residual_ref, normed_ref, gates_ref, cot_ref = refs[groups : groups + 5]
    routes_ref, slot_ref, drop_ref = refs[groups + 5 : groups + 8]
    out_ref, gres_ref, gresb_ref, small_ref = refs[groups + 8 :]
    count, width = cot_ref.shape
    places = places_of(routes_ref, slot_ref, drop_ref, experts * CAP)
    onehot = route_onehot(routes_ref, experts)
    keep = (1 - drop_ref[...]).astype(F32)
    gates = [gates_ref[:, 0:1], gates_ref[:, 1:2]]
    up = cot_ref[...].astype(F32)
    residual = residual_ref[...]
    values = back_ref[:, :width]
    picked = [dot_nn(p, values) for p in places]
    moe = gates[0] * keep[:, 0:1] * picked[0] + gates[1] * keep[:, 1:2] * picked[1]
    out_ref[...] = (residual + moe).astype(BF16)
    gg = [keep[:, r : r + 1] * jnp.sum(up * picked[r], axis=1, keepdims=True) for r in range(2)]
    mean = gates[0] * gg[0] + gates[1] * gg[1]
    gc = [gates[r] * (gg[r] - mean) for r in range(2)]
    glog = (onehot[0] * gc[0] + onehot[1] * gc[1]).astype(BF16)
    extra = sum_refs(ext)
    gain = extra[13:14, :]
    router = extra[16 : 16 + experts, :].astype(BF16)
    gn = dot_nn(places[0] + places[1], back_ref[:, width:]) + dot_nn(glog, router)
    scale = norm_scale(residual)
    small_ref[0:experts, :] = dot_tn(glog, normed_ref[...])
    small_ref[experts : experts + 8, :] = jnp.broadcast_to(
        jnp.sum(gn * residual * scale, axis=0, keepdims=True), (8, width)
    )
    scaled = gn * gain
    inner = jnp.mean(scaled * residual, axis=-1, keepdims=True)
    gres = up + scale * scaled - residual * (scale * scale * scale * inner)
    gres_ref[...] = gres
    gresb_ref[...] = gres.astype(BF16)


def mixer_kernel(groups, heads, hs, me_ref, *refs):
    gr = refs[:groups]
    wo_ref, mixed_ref, proj_ref, lse_ref, tile_ref, far_ref = refs[groups : groups + 6]
    gpo_ref, gproj_ref, buckets_ref, grf_ref, gm_ref = refs[groups + 6 :]
    me = me_ref[0]
    count = gr[0].shape[0]
    length = count * groups
    for k in range(groups):
        grf_ref[rows_at(me ^ k, count), :] = gr[k][...]
    gpo_ref[...] = dot_tn(mixed_ref[...], grf_ref[...]).astype(BF16)
    gm_ref[...] = dot_nt(grf_ref[...], wo_ref[...]).astype(BF16)
    factor = hs ** (-0.5)
    part = heads * hs
    blocks_n = length // BLOCK
    distance = distance_tile()
    dqs = [[None] * heads for _ in range(blocks_n)]
    dks = [[None] * heads for _ in range(blocks_n)]
    dvs = [[None] * heads for _ in range(blocks_n)]
    for h in range(heads):
        near = jnp.zeros((BLOCK, BLOCK), F32)
        prev = jnp.zeros((BLOCK, BLOCK), F32)
        rest = jnp.zeros((BLOCK, BLOCK), F32)
        for qb in range(blocks_n):
            span = slice(qb * BLOCK, (qb + 1) * BLOCK)
            keys = (qb + 1) * BLOCK
            q = proj_ref[span, h * hs : (h + 1) * hs]
            k = proj_ref[:keys, part + h * hs : part + (h + 1) * hs]
            v = proj_ref[:keys, 2 * part + h * hs : 2 * part + (h + 1) * hs]
            gm = gm_ref[span, h * hs : (h + 1) * hs]
            lse = lse_ref[span, h : h + 1]
            blocks = score_blocks(q, k, tile_ref[h], far_ref[h, 0:1, 0:1], qb, factor)
            ps = [jnp.exp(s - lse) for s in blocks]
            gws = [dot_nt(gm, v[kb * BLOCK : (kb + 1) * BLOCK]) for kb in range(qb + 1)]
            inner = ps[0] * gws[0]
            for kb in range(1, qb + 1):
                inner = inner + ps[kb] * gws[kb]
            inner = jnp.sum(inner, axis=-1, keepdims=True)
            ds = [ps[kb] * (gws[kb] - inner) for kb in range(qb + 1)]
            near = near + ds[qb]
            if qb >= 1:
                prev = prev + ds[qb - 1]
            for kb in range(qb - 1):
                rest = rest + ds[kb]
            dsb = jnp.concatenate([d.astype(BF16) for d in ds], axis=1)
            pb = jnp.concatenate([p.astype(BF16) for p in ps], axis=1)
            dqs[qb][h] = dot_nn(dsb, k) * factor
            dk = dot_tn(dsb, q)
            dv = dot_tn(pb, gm)
            for kb in range(qb + 1):
                cut = slice(kb * BLOCK, (kb + 1) * BLOCK)
                if dks[kb][h] is None:
                    dks[kb][h], dvs[kb][h] = dk[cut], dv[cut]
                else:
                    dks[kb][h] = dks[kb][h] + dk[cut]
                    dvs[kb][h] = dvs[kb][h] + dv[cut]
        tile = jnp.concatenate([prev, near], axis=1)
        far = jnp.sum(rest, axis=0, keepdims=True)
        far = jnp.concatenate([far, jnp.zeros_like(far)], axis=1)
        sums = []
        for n in range(NB):
            inside = distance >= STARTS[n]
            if n + 1 < NB:
                inside = inside & (distance < STARTS[n + 1])
            one = jnp.sum(jnp.where(inside, tile, 0.0), axis=0, keepdims=True)
            sums.append(one + far if n == NB - 1 else one)
        buckets_ref[h] = jnp.concatenate(sums, axis=0)
    for b in range(blocks_n):
        span = slice(b * BLOCK, (b + 1) * BLOCK)
        full = jnp.concatenate(dqs[b] + [d * factor for d in dks[b]] + dvs[b], axis=1)
        gproj_ref[span, :] = full.astype(BF16)


def project_kernel(groups, slots, me_ref, *refs):
    tok = refs[:groups]
    gproj_ref, normed_ref, wfull_ref = refs[groups : groups + 3]
    gpi_ref, send_ref, keep_ref, mid_ref, gain_ref, gi_ref, gn_ref = refs[groups + 3 :]
    me = me_ref[0]
    pos = me_ref[1]
    count, width = tok[0].shape
    gi_ref[...] = dot_tn(normed_ref[...], gproj_ref[...])
    if slots == 0:
        gpi_ref[...] = gi_ref[...].astype(BF16)
    else:
        block = width // groups
        rows = block // slots
        for s in range(slots):
            parts = [
                gi_ref[pl.ds(pl.multiple_of((me ^ t) * block + (pos ^ s) * rows, 8), rows), :]
                for t in range(groups)
            ]
            gpi_ref[s] = jnp.concatenate(parts, axis=0).astype(BF16)
    gn_ref[...] = dot_nt(gproj_ref[...], wfull_ref[...])
    total = jnp.zeros((1, width), F32)
    for k in range(groups):
        x = tok[k][...].astype(F32)
        gn = gn_ref[rows_at(me ^ k, count), :]
        total = total + jnp.sum(gn * (x * norm_scale(x)), axis=0, keepdims=True)
        if k == 0:
            keep_ref[...] = gn
        elif k == 2:
            mid_ref[...] = gn
        elif k == 1:
            send_ref[0:count, :] = gn.astype(BF16)
        else:
            send_ref[count : 2 * count, :] = gn.astype(BF16)
    gain_ref[...] = jnp.broadcast_to(total, (8, width))


def final_kernel(groups, slots, me_ref, src_ref, out_ref, full_ref):
    me = me_ref[0]
    pos = me_ref[1]
    full_ref[...] = src_ref[...].astype(F32)
    rows = out_ref.shape[0] // slots
    third = out_ref.shape[1] // 3
    part = third // groups
    for s in range(slots):
        for w in range(groups):
            piece = full_ref[s, pl.ds(pl.multiple_of((me ^ w) * rows, 8), rows), :]
            target = pl.ds(pl.multiple_of((pos ^ s) * rows, 8), rows)
            for i in range(3):
                out_ref[target, i * third + w * part : i * third + (w + 1) * part] = piece[
                    :, i * part : (i + 1) * part
                ]


def halve(value, axis):
    bit = 1
    size = lax.axis_size(axis)
    while bit < size:
        pairs = value.reshape((value.shape[0] // 2, 2) + value.shape[1:])
        got = exchange(pairs[:, 1], axis, bit)
        value = (pairs[:, 0].astype(F32) + got.astype(F32)).astype(BF16)
        bit *= 2
    return value


def double(value, axis):
    bit = lax.axis_size(axis) // 2
    while bit >= 1:
        got = exchange(value, axis, bit)
        value = jnp.stack([value, got], axis=1).reshape((-1,) + value.shape[1:])
        bit //= 2
    return value


def sum_all(value, axes):
    for axis in axes:
        bit = 1
        while bit < lax.axis_size(axis):
            value = value + exchange(value, axis, bit)
            bit *= 2
    return value


def reduce_rows(send, keep, mid, axis):
    rows = keep.shape[0]
    got = exchange(send, axis, 1).astype(F32)
    other = (mid + got[rows:]).astype(BF16)
    return keep + got[:rows] + exchange(other, axis, 2).astype(F32)


def body(
    tokens,
    gain_attention,
    gain_experts,
    proj_inputs,
    proj_output,
    bias_table,
    router_weight,
    routes,
    slot_index,
    drop_flags,
    expert_in,
    expert_out,
    cotangent,
):
    groups = lax.axis_size("wshard")
    size = lax.axis_size("expert")
    me = lax.axis_index("wshard")
    pos = lax.axis_index("expert")
    where = jnp.stack([me, pos]).astype(jnp.int32)
    count, width = tokens.shape
    length = count * groups
    heads_all = bias_table.shape[1]
    heads = heads_all // groups
    hs = width // heads_all
    part = width // groups
    local = expert_in.shape[0]
    experts = local * size
    hidden_local = expert_in.shape[2]
    buckets = bias_table.shape[0] * groups

    extra_rows = 16 + experts
    small = jnp.zeros((extra_rows, width), BF16)
    small = lax.dynamic_update_slice(small, bias_table.T, (0, me * bias_table.shape[0]))
    small = lax.dynamic_update_slice(
        small, jnp.stack([gain_attention, gain_experts]), (12, me * part)
    )
    small = lax.dynamic_update_slice(small, router_weight.T, (16, me * part))

    tok = gather_xor(tokens, "wshard")
    chunks = whole(
        lambda *r: prepare_kernel(groups, *r),
        [((part, 3 * part), BF16)] * groups,
        where,
        proj_inputs,
        scratch=[pltpu.VMEM((groups, part, 3 * part), BF16)],
    )
    wp = [chunks[0]] + [exchange(chunks[k], "wshard", k) for k in range(1, groups)]
    ext = gather_xor(small, "wshard")
    own_output = lax.optimization_barrier((proj_output, wp[-1]))[0]
    wo = gather_xor(own_output, "wshard")

    front = whole(
        lambda *r: front_kernel(groups, heads, hs, *r),
        [
            ((length, width), BF16),
            ((width, 3 * part), BF16),
            ((length, 3 * part), BF16),
            ((length, part), BF16),
            ((length, 128), F32),
            ((heads, BLOCK, 2 * BLOCK), F32),
            ((heads, 8, 128), F32),
        ]
        + [((count, part), BF16)] * groups,
        where,
        *tok,
        *wp,
        *ext,
        scratch=[pltpu.VMEM((extra_rows, width), F32)],
    )
    normed_one, wfull, projected, mixed, lse, tile, far = front[:7]
    mine = front[7:]
    pieces = [mine[0]] + [exchange(mine[k], "wshard", k) for k in range(1, groups)]

    slots = experts * CAP
    residual, normed_two, send, gates = whole(
        lambda *r: middle_kernel(groups, experts, *r),
        [
            ((count, width), F32),
            ((count, width), BF16),
            ((slots, 2 * width), BF16),
            ((count, 128), F32),
        ],
        *pieces,
        *wo,
        *ext,
        tokens,
        cotangent,
        routes,
        slot_index,
        drop_flags,
        smem=0,
    )
    sent = lax.all_to_all(
        send.reshape(size, local * CAP, 2 * width), "expert", 0, 0, tiled=True
    ).reshape(slots, 2 * width)
    xs = gather_xor(sent, "wshard")

    rows = slots * groups
    fblock = 256
    steps = hidden_local // fblock
    full = pl.BlockSpec((slots, 2 * width), lambda f: (0, 0))
    hidden, gpre, back_send, back_keep, back_mid = pl.pallas_call(
        lambda *r: experts_kernel(groups, local, *r),
        grid=(steps,),
        in_specs=[full] * groups
        + [
            pl.BlockSpec((local, width, fblock), lambda f: (0, 0, f)),
            pl.BlockSpec((local, fblock, width), lambda f: (0, f, 0)),
        ],
        out_specs=[
            pl.BlockSpec((rows, fblock), lambda f: (0, f)),
            pl.BlockSpec((rows, fblock), lambda f: (0, f)),
            pl.BlockSpec((2 * slots, 2 * width), lambda f: (0, 0)),
            pl.BlockSpec((slots, 2 * width), lambda f: (0, 0)),
            pl.BlockSpec((slots, 2 * width), lambda f: (0, 0)),
        ],
        out_shape=[
            jax.ShapeDtypeStruct((rows, hidden_local), BF16),
            jax.ShapeDtypeStruct((rows, hidden_local), BF16),
            jax.ShapeDtypeStruct((2 * slots, 2 * width), BF16),
            jax.ShapeDtypeStruct((slots, 2 * width), F32),
            jax.ShapeDtypeStruct((slots, 2 * width), F32),
        ],
        scratch_shapes=[
            pltpu.VMEM((rows, 2 * width), BF16),
            pltpu.VMEM((rows, 2 * width), F32),
        ],
    )(*xs, expert_in, expert_out)

    full2 = pl.BlockSpec((slots, 2 * width), lambda j, f: (0, 0))
    grad_expert_in, grad_expert_out = pl.pallas_call(
        lambda *r: weights_kernel(groups, local, *r),
        grid=(local, steps),
        in_specs=[full2] * groups
        + [
            pl.BlockSpec((rows, fblock), lambda j, f: (0, f)),
            pl.BlockSpec((rows, fblock), lambda j, f: (0, f)),
        ],
        out_specs=[
            pl.BlockSpec((1, width, fblock), lambda j, f: (j, 0, f)),
            pl.BlockSpec((1, fblock, width), lambda j, f: (j, f, 0)),
        ],
        out_shape=[
            jax.ShapeDtypeStruct(expert_in.shape, F32),
            jax.ShapeDtypeStruct(expert_out.shape, F32),
        ],
        scratch_shapes=[pltpu.VMEM((rows, 2 * width), BF16)],
    )(*xs, hidden, gpre)

    returned = reduce_rows(back_send, back_keep, back_mid, "wshard").astype(BF16)
    returned = lax.all_to_all(
        returned.reshape(size, local * CAP, 2 * width), "expert", 0, 0, tiled=True
    ).reshape(slots, 2 * width)

    output, grad_residual, grad_res_b, early = whole(
        lambda *r: return_kernel(groups, experts, *r),
        [
            ((count, width), BF16),
            ((count, width), F32),
            ((count, width), BF16),
            ((experts + 8, width), F32),
        ],
        *ext,
        returned,
        residual,
        normed_two,
        gates,
        cotangent,
        routes,
        slot_index,
        drop_flags,
        smem=0,
    )
    gr = gather_xor(grad_res_b, "wshard")
    gpo, gproj, bucket_sums = whole(
        lambda *r: mixer_kernel(groups, heads, hs, *r),
        [
            ((part, width), BF16),
            ((length, 3 * part), BF16),
            ((heads, NB, 2 * BLOCK), F32),
        ],
        where,
        *gr,
        proj_output,
        mixed,
        projected,
        lse,
        tile,
        far,
        scratch=[pltpu.VMEM((length, width), BF16), pltpu.VMEM((length, part), BF16)],
    )
    fast = part % (8 * size) == 0
    cuts = size if fast else 0
    gpi_shape = (size, width // size, 3 * part) if fast else (width, 3 * part)
    gpi, gn_send, gn_keep, gn_mid, gain_one = whole(
        lambda *r: project_kernel(groups, cuts, *r),
        [
            (gpi_shape, BF16),
            ((2 * count, width), BF16),
            ((count, width), F32),
            ((count, width), F32),
            ((8, width), F32),
        ],
        where,
        *tok,
        gproj,
        normed_one,
        wfull,
        scratch=[pltpu.VMEM((width, 3 * part), F32), pltpu.VMEM((length, width), F32)],
    )
    grad_normed_one = reduce_rows(gn_send, gn_keep, gn_mid, "wshard")
    inputs = tokens.astype(F32)
    scale_one = norm_scale(inputs)
    gain_one_f = sum(e[12:13].astype(F32) for e in ext)
    scaled = grad_normed_one * gain_one_f
    inner = jnp.mean(scaled * inputs, axis=-1, keepdims=True)
    grad_tokens = grad_residual + (
        scale_one * scaled - inputs * scale_one * scale_one * scale_one * inner
    )

    table_rows = jnp.sum(bucket_sums, axis=-1)
    late = jnp.zeros((16, width), F32)
    late = lax.dynamic_update_slice(late, table_rows, (me * heads, 0))
    late = lax.dynamic_update_slice(late, gain_one[0:1], (12, 0))
    early = sum_all(early, ("wshard", "expert"))
    late = sum_all(late, ("wshard", "expert"))
    grad_router = lax.dynamic_slice(early[:experts], (0, me * part), (experts, part)).T
    grad_gain_two = lax.dynamic_slice(early[experts], (me * part,), (part,))
    grad_gain_one = lax.dynamic_slice(late[12], (me * part,), (part,))
    per = buckets // groups
    grad_table = lax.dynamic_slice(late, (0, me * per), (heads_all, per)).T

    if fast:
        out_cut = gpo.reshape(size, part // size, width)
        out_cut = jnp.stack([out_cut[pos ^ s] for s in range(size)])
        out_sum = double(halve(out_cut, "expert"), "expert")
        total_output = jnp.stack([out_sum[pos ^ s] for s in range(size)])
        total_output = total_output.reshape(part, width).astype(F32)
        mine = halve(gpi, "expert")[0]
        step = part // size
        cut = [mine[t * step : (t + 1) * step] for t in range(groups)]
        cut = [cut[0]] + [exchange(cut[t], "wshard", t) for t in range(1, groups)]
        every = double(jnp.concatenate(cut, axis=0)[None], "expert")
        total_inputs = whole(
            lambda *r: final_kernel(groups, size, *r),
            [((part, 3 * width), F32)],
            where,
            every,
            scratch=[pltpu.VMEM(every.shape, F32)],
        )[0]
    else:
        total_output = lax.psum(gpo.astype(F32), "expert")
        total = lax.psum(gpi, "expert").reshape(groups, part, 3, part)
        total = lax.all_to_all(total, "wshard", 0, 0, tiled=True)
        total_inputs = total.transpose(1, 2, 0, 3).reshape(part, 3 * width).astype(F32)
    return (
        output,
        grad_tokens,
        grad_gain_one,
        grad_gain_two,
        total_inputs,
        total_output,
        grad_table,
        grad_router,
        grad_expert_in,
        grad_expert_out,
    )


def solution(mesh):
    placed = (
        P(("expert", "wshard"), None),
        P("wshard"),
        P("wshard"),
        P("wshard", None),
        P("wshard", None),
        P("wshard", None),
        P("wshard", None),
        P(("expert", "wshard"), None),
        P(("expert", "wshard"), None),
        P(("expert", "wshard"), None),
        P("expert", None, "wshard"),
        P("expert", "wshard", None),
        P(("expert", "wshard"), None),
    )
    return jax.shard_map(
        body,
        mesh=mesh,
        in_specs=placed,
        out_specs=(
            P(("expert", "wshard"), None),
            P(("expert", "wshard"), None),
            P("wshard"),
            P("wshard"),
            P("wshard", None),
            P("wshard", None),
            P("wshard", None),
            P("wshard", None),
            P("expert", None, "wshard"),
            P("expert", "wshard", None),
        ),
        check_vma=False,
    )
```

```python
import math

import jax
import jax.numpy as jnp
from jax import lax
from jax.experimental import pallas as pl
from jax.experimental.pallas import tpu as pltpu
from jax.sharding import PartitionSpec as P


NB = 32
MAXDIST = 128
CAP = 4
EPSILON = 1e-06
NEGATIVE = -1e30
BLOCK = 128
F32 = jnp.float32
BF16 = jnp.bfloat16


def bucket_starts():
    exact = NB // 2
    starts = list(range(exact + 1))
    for level in range(1, exact):
        starts.append(math.ceil(exact * (MAXDIST / exact) ** (level / exact) - 1e-09))
    return starts


STARTS = bucket_starts()


def exchange(value, axis, mask):
    size = lax.axis_size(axis)
    return lax.ppermute(value, axis, [(i, i ^ mask) for i in range(size)])


def gather_xor(value, axis):
    pieces = {0: value}
    bit = lax.axis_size(axis) // 2
    while bit >= 1:
        for key in list(pieces):
            pieces[key | bit] = exchange(pieces[key], axis, bit)
        bit //= 2
    return [pieces[k] for k in range(len(pieces))]


def whole(kernel, outs, *args, scratch=(), smem=1):
    return call_whole(kernel, outs, *args, scratch=scratch, smem=smem)


def call_whole(kernel, outs, *args, scratch, smem):
    specs = [pl.BlockSpec(memory_space=pltpu.SMEM)] * smem
    specs += [pl.BlockSpec(memory_space=pltpu.VMEM)] * (len(args) - smem)
    return pl.pallas_call(
        kernel,
        out_shape=[jax.ShapeDtypeStruct(s, d) for s, d in outs],
        in_specs=specs,
        out_specs=[pl.BlockSpec(memory_space=pltpu.VMEM)] * len(outs),
        scratch_shapes=list(scratch),
    )(*args)


def dot_nn(a, b):
    return lax.dot_general(a, b, (((1,), (0,)), ((), ())), preferred_element_type=F32)


def dot_nt(a, b):
    return lax.dot_general(a, b, (((1,), (1,)), ((), ())), preferred_element_type=F32)


def dot_tn(a, b):
    return lax.dot_general(a, b, (((0,), (0,)), ((), ())), preferred_element_type=F32)


def norm_scale(values):
    return lax.rsqrt(jnp.mean(values * values, axis=-1, keepdims=True) + EPSILON)


def sum_refs(refs):
    total = refs[0][...].astype(F32)
    for ref in refs[1:]:
        total = total + ref[...].astype(F32)
    return total


def distance_tile():
    rows = lax.broadcasted_iota(jnp.int32, (BLOCK, 2 * BLOCK), 0)
    cols = lax.broadcasted_iota(jnp.int32, (BLOCK, 2 * BLOCK), 1)
    return rows + BLOCK - cols


def rows_at(index, size):
    return pl.ds(pl.multiple_of(index * size, size & -size), size)


def prepare_kernel(groups, me_ref, w_ref, *outs_and_scratch):
    outs = outs_and_scratch[:groups]
    chunks = outs_and_scratch[groups]
    me = me_ref[0]
    third = w_ref.shape[1] // 3
    part = third // groups
    for d in range(groups):
        for s in range(3):
            chunks[d, :, s * part : (s + 1) * part] = w_ref[
                :, s * third + d * part : s * third + (d + 1) * part
            ]
    for k in range(groups):
        outs[k][...] = chunks[me ^ k]


def score_blocks(q, k, tile, far, qb, factor):
    blocks = []
    for kb in range(qb + 1):
        s = dot_nt(q, k[kb * BLOCK : (kb + 1) * BLOCK]) * factor
        if kb == qb:
            s = s + tile[:, BLOCK:]
        elif kb == qb - 1:
            s = s + tile[:, :BLOCK]
        else:
            s = s + far
        blocks.append(s)
    return blocks


def front_kernel(groups, heads, hs, me_ref, *refs):
    tok = refs[:groups]
    wp = refs[groups : 2 * groups]
    ext = refs[2 * groups : 3 * groups]
    outs = refs[3 * groups :]
    normed_ref, wfull_ref, proj_ref, mixed_ref, prob_ref = outs[:5]
    pieces = outs[5 : 5 + groups]
    tab_ref = outs[5 + groups]
    me = me_ref[0]
    count = tok[0].shape[0]
    wrows = wp[0].shape[0]
    length = count * groups
    extra = sum_refs(ext)
    gain = extra[12:13, :]
    tab_ref[...] = extra
    for k in range(groups):
        x = tok[k][...].astype(F32)
        normed_ref[rows_at(me ^ k, count), :] = (x * norm_scale(x) * gain).astype(BF16)
        wfull_ref[rows_at(me ^ k, wrows), :] = wp[k][...]
    proj_ref[...] = dot_nn(normed_ref[...], wfull_ref[...]).astype(BF16)
    distance = distance_tile()
    factor = hs ** (-0.5)
    part = heads * hs
    tiles = []
    fars = []
    for h in range(heads):
        row = tab_ref[pl.ds(me * heads + h, 1), :]
        tile = jnp.broadcast_to(row[:, 0:1], distance.shape)
        for n in range(1, NB):
            tile = jnp.where(distance >= STARTS[n], row[:, n : n + 1], tile)
        tiles.append(jnp.where(distance >= 0, tile, NEGATIVE))
        fars.append(row[:, NB - 1 : NB])
    for qb in range(length // BLOCK):
        span = slice(qb * BLOCK, (qb + 1) * BLOCK)
        keys = (qb + 1) * BLOCK
        mixed = []
        for h in range(heads):
            q = proj_ref[span, h * hs : (h + 1) * hs]
            k = proj_ref[:keys, part + h * hs : part + (h + 1) * hs]
            v = proj_ref[:keys, 2 * part + h * hs : 2 * part + (h + 1) * hs]
            blocks = score_blocks(q, k, tiles[h], fars[h], qb, factor)
            top = blocks[0]
            for s in blocks[1:]:
                top = jnp.maximum(top, s)
            top = jnp.max(top, axis=-1, keepdims=True)
            es = [jnp.exp(s - top) for s in blocks]
            total = es[0]
            for e in es[1:]:
                total = total + e
            total = jnp.sum(total, axis=-1, keepdims=True)
            inverse = 1.0 / total
            w = jnp.concatenate([e * inverse for e in es], axis=1)
            prob_ref[h, span, :keys] = w
            mixed.append(dot_nn(w.astype(BF16), v))
        mixed_ref[span, :] = jnp.concatenate(mixed, axis=1).astype(BF16)
    for k in range(groups):
        pieces[k][...] = mixed_ref[rows_at(me ^ k, count), :]


def columns(table_ref):
    table = jnp.transpose(table_ref[...])
    return [table[:, i : i + 1] for i in range(6)]


def places_of(cols, slots):
    ids = lax.broadcasted_iota(jnp.int32, (cols[0].shape[0], slots), 1).astype(F32)
    flat = [cols[r] * float(CAP) + cols[2 + r] for r in range(2)]
    flat = [jnp.where(cols[4 + r] == 0.0, flat[r], -1.0) for r in range(2)]
    return [(f == ids).astype(F32).astype(BF16) for f in flat]


def route_onehot(cols, experts):
    ids = lax.broadcasted_iota(jnp.int32, (cols[0].shape[0], experts), 1).astype(F32)
    return [(cols[r] == ids).astype(F32) for r in range(2)]


def middle_kernel(groups, experts, *refs):
    mixed = refs[:groups]
    wo = refs[groups : 2 * groups]
    ext = refs[2 * groups : 3 * groups]
    tok_ref, cot_ref, table_ref = refs[3 * groups : 3 * groups + 3]
    residual_ref, normed_ref, send_ref, gates_ref = refs[3 * groups + 3 :]
    cols = columns(table_ref)
    count, width = tok_ref.shape
    total = dot_nn(mixed[0][...], wo[0][...])
    for k in range(1, groups):
        total = total + dot_nn(mixed[k][...], wo[k][...])
    residual = tok_ref[...].astype(F32) + total
    residual_ref[...] = residual
    extra = sum_refs(ext)
    gain = extra[13:14, :]
    router = extra[16 : 16 + experts, :].astype(BF16)
    normed = (residual * norm_scale(residual) * gain).astype(BF16)
    normed_ref[...] = normed
    logits = dot_nt(normed, router)
    onehot = route_onehot(cols, experts)
    chosen = [jnp.sum(logits * o, axis=1, keepdims=True) for o in onehot]
    top = jnp.maximum(chosen[0], chosen[1])
    ex = [jnp.exp(c - top) for c in chosen]
    both = ex[0] + ex[1]
    gates = [e / both for e in ex]
    keep = [1.0 - cols[4], 1.0 - cols[5]]
    places = places_of(cols, experts * CAP)
    up = cot_ref[...].astype(F32)
    send_ref[:, :width] = dot_tn(places[0] + places[1], normed).astype(BF16)
    grads = dot_tn(places[0], (gates[0] * keep[0] * up).astype(BF16))
    grads = grads + dot_tn(places[1], (gates[1] * keep[1] * up).astype(BF16))
    send_ref[:, width:] = grads.astype(BF16)
    lanes = lax.broadcasted_iota(jnp.int32, (count, 128), 1)
    gates_ref[...] = jnp.where(lanes == 0, gates[0], gates[1])


def owner_mask(rows, local, j):
    index = lax.broadcasted_iota(jnp.int32, (rows, 1), 0)
    return (index // CAP) % local == j


def experts_kernel(groups, local, *refs):
    xs = refs[:groups]
    win_ref, wout_ref = refs[groups : groups + 2]
    hidden_ref, gpre_ref, send_ref, keep_ref, mid_ref, x_ref, acc_ref = refs[groups + 2 :]
    step = pl.program_id(0)
    rows = xs[0].shape[0]
    width = xs[0].shape[1] // 2

    @pl.when(step == 0)
    def _():
        for k in range(groups):
            x_ref[k * rows : (k + 1) * rows, :] = xs[k][...]
        acc_ref[...] = jnp.zeros_like(acc_ref)

    r = x_ref[:, :width]
    g = x_ref[:, width:]
    masks = [owner_mask(rows * groups, local, j) for j in range(local)]
    pre = dot_nn(r, win_ref[0])
    gh = dot_nt(g, wout_ref[0])
    for j in range(1, local):
        pre = jnp.where(masks[j], dot_nn(r, win_ref[j]), pre)
        gh = jnp.where(masks[j], dot_nt(g, wout_ref[j]), gh)
    root = math.sqrt(2.0 / math.pi)
    square = pre * pre
    th = jnp.tanh(root * (pre + 0.044715 * (square * pre)))
    cdf = 0.5 * (1.0 + th)
    hid = pre * cdf
    slope = cdf + 0.5 * pre * (1.0 - th * th) * (root * (1.0 + 3.0 * 0.044715 * square))
    gp = gh * slope
    hidden_ref[...] = hid.astype(BF16)
    gpre_ref[...] = gp.astype(BF16)
    for j in range(local):
        acc_ref[:, :width] += dot_nn(jnp.where(masks[j], hid, 0.0).astype(BF16), wout_ref[j])
        acc_ref[:, width:] += dot_nt(jnp.where(masks[j], gp, 0.0).astype(BF16), win_ref[j])

    @pl.when(step == pl.num_programs(0) - 1)
    def _():
        keep_ref[...] = acc_ref[0:rows, :]
        mid_ref[...] = acc_ref[2 * rows : 3 * rows, :]
        send_ref[0:rows, :] = acc_ref[rows : 2 * rows, :].astype(BF16)
        send_ref[rows : 2 * rows, :] = acc_ref[3 * rows : 4 * rows, :].astype(BF16)


def weights_kernel(groups, local, *refs):
    xs = refs[:groups]
    hidden_ref, gpre_ref, gin_ref, gout_ref, x_ref = refs[groups:]
    j = pl.program_id(0)
    rows = xs[0].shape[0]
    width = xs[0].shape[1] // 2

    @pl.when(pl.program_id(1) == 0)
    def _():
        for k in range(groups):
            x_ref[k * rows : (k + 1) * rows, :] = xs[k][...]

    mask = owner_mask(rows * groups, local, j)
    gp = jnp.where(mask, gpre_ref[...].astype(F32), 0.0).astype(BF16)
    hid = jnp.where(mask, hidden_ref[...].astype(F32), 0.0).astype(BF16)
    gin_ref[0] = dot_tn(x_ref[:, :width], gp)
    gout_ref[0] = dot_tn(hid, x_ref[:, width:])


def return_kernel(groups, experts, *refs):
    ext = refs[:groups]
    back_ref, residual_ref, normed_ref, gates_ref, cot_ref = refs[groups : groups + 5]
    table_ref = refs[groups + 5]
    out_ref, gres_ref, gresb_ref, small_ref = refs[groups + 6 :]
    cols = columns(table_ref)
    _, width = cot_ref.shape
    places = places_of(cols, experts * CAP)
    onehot = route_onehot(cols, experts)
    keep = [1.0 - cols[4], 1.0 - cols[5]]
    gates = [gates_ref[:, 0:1], gates_ref[:, 1:2]]
    up = cot_ref[...].astype(F32)
    residual = residual_ref[...]
    values = back_ref[:, :width]
    picked = [dot_nn(p, values) for p in places]
    moe = gates[0] * keep[0] * picked[0] + gates[1] * keep[1] * picked[1]
    out_ref[...] = (residual + moe).astype(BF16)
    gg = [keep[r] * jnp.sum(up * picked[r], axis=1, keepdims=True) for r in range(2)]
    mean = gates[0] * gg[0] + gates[1] * gg[1]
    gc = [gates[r] * (gg[r] - mean) for r in range(2)]
    glog = (onehot[0] * gc[0] + onehot[1] * gc[1]).astype(BF16)
    extra = sum_refs(ext)
    gain = extra[13:14, :]
    router = extra[16 : 16 + experts, :].astype(BF16)
    gn = dot_nn(places[0] + places[1], back_ref[:, width:]) + dot_nn(glog, router)
    scale = norm_scale(residual)
    small_ref[0:16, :] = jnp.zeros((16, width), F32)
    small_ref[13:14, :] = jnp.sum(gn * residual * scale, axis=0, keepdims=True)
    small_ref[16 : 16 + experts, :] = dot_tn(glog, normed_ref[...])
    scaled = gn * gain
    inner = jnp.mean(scaled * residual, axis=-1, keepdims=True)
    gres = up + scale * scaled - residual * (scale * scale * scale * inner)
    gres_ref[...] = gres
    gresb_ref[...] = gres.astype(BF16)


def slot_rows(ref, block, rows, me, pos, t, s):
    return ref[pl.ds(pl.multiple_of((me ^ t) * block + (pos ^ s) * rows, 8), rows), :]


def values_kernel(groups, heads, hs, slots, me_ref, *refs):
    gr = refs[:groups]
    wo_ref, mixed_ref, prob_ref, normed_ref = refs[groups : groups + 4]
    gm_ref, gv_ref, send_ref, keep_ref, grf_ref, go_ref, gi_ref = refs[groups + 4 :]
    me = me_ref[0]
    pos = me_ref[1]
    count = gr[0].shape[0]
    length = count * groups
    for k in range(groups):
        grf_ref[rows_at(me ^ k, count), :] = gr[k][...]
    gm_ref[...] = dot_nt(grf_ref[...], wo_ref[...]).astype(BF16)
    go_ref[...] = dot_tn(mixed_ref[...], grf_ref[...])
    for b in range(length // BLOCK):
        cut = slice(b * BLOCK, (b + 1) * BLOCK)
        dv = [
            dot_tn(
                prob_ref[h, b * BLOCK :, cut].astype(BF16),
                gm_ref[b * BLOCK :, h * hs : (h + 1) * hs],
            )
            for h in range(heads)
        ]
        gv_ref[cut, :] = jnp.concatenate(dv, axis=1).astype(BF16)
    gi_ref[...] = dot_tn(normed_ref[...], gv_ref[...])
    if slots == 0:
        send_ref[...] = go_ref[...].astype(BF16)
        keep_ref[...] = gi_ref[...].astype(BF16)
        return
    block = go_ref.shape[0]
    rows = block // slots
    for s in range(slots):
        own = go_ref[pl.ds(pl.multiple_of((pos ^ s) * rows, 8), rows), :]
        parts = [slot_rows(gi_ref, block, rows, me, pos, t, s) for t in range(groups)]
        both = jnp.concatenate([own, jnp.concatenate(parts, axis=1)], axis=0).astype(BF16)
        if s % 2:
            send_ref[s // 2] = both
        else:
            keep_ref[s // 2] = both


def scores_kernel(groups, heads, hs, slots, me_ref, *refs):
    tok = refs[:groups]
    gm_ref, gv_ref, proj_ref, prob_ref, normed_ref, wfull_ref = refs[groups : groups + 6]
    early_ref = refs[groups + 6]
    outs = refs[groups + 7 :]
    send_ref, keep_ref, rows_ref, own_ref, mid_ref, small_ref = outs[:6]
    gproj_ref, gi_ref, gn_ref = outs[6:]
    me = me_ref[0]
    pos = me_ref[1]
    count, width = tok[0].shape
    length = count * groups
    factor = hs ** (-0.5)
    part = heads * hs
    blocks_n = length // BLOCK
    distance = distance_tile()
    dqs = [[None] * heads for _ in range(blocks_n)]
    dks = [[None] * heads for _ in range(blocks_n)]
    tiles = []
    for h in range(heads):
        near = jnp.zeros((BLOCK, BLOCK), F32)
        prev = jnp.zeros((BLOCK, BLOCK), F32)
        rest = jnp.zeros((BLOCK, BLOCK), F32)
        for qb in range(blocks_n):
            span = slice(qb * BLOCK, (qb + 1) * BLOCK)
            keys = (qb + 1) * BLOCK
            q = proj_ref[span, h * hs : (h + 1) * hs]
            k = proj_ref[:keys, part + h * hs : part + (h + 1) * hs]
            v = proj_ref[:keys, 2 * part + h * hs : 2 * part + (h + 1) * hs]
            gm = gm_ref[span, h * hs : (h + 1) * hs]
            p = prob_ref[h, span, :keys]
            gw = dot_nt(gm, v)
            inner = jnp.sum(p * gw, axis=-1, keepdims=True)
            ds = p * (gw - inner)
            near = near + ds[:, qb * BLOCK :]
            if qb >= 1:
                prev = prev + ds[:, (qb - 1) * BLOCK : qb * BLOCK]
            for kb in range(qb - 1):
                rest = rest + ds[:, kb * BLOCK : (kb + 1) * BLOCK]
            dsb = ds.astype(BF16)
            dqs[qb][h] = dot_nn(dsb, k) * factor
            dk = dot_tn(dsb, q)
            for kb in range(qb + 1):
                cut = slice(kb * BLOCK, (kb + 1) * BLOCK)
                if dks[kb][h] is None:
                    dks[kb][h] = dk[cut]
                else:
                    dks[kb][h] = dks[kb][h] + dk[cut]
        tiles.append((jnp.concatenate([prev, near], axis=1), rest))
    for b in range(blocks_n):
        span = slice(b * BLOCK, (b + 1) * BLOCK)
        full = jnp.concatenate(dqs[b] + [d * factor for d in dks[b]], axis=1)
        gproj_ref[span, : 2 * part] = full.astype(BF16)
    gproj_ref[:, 2 * part :] = gv_ref[...]
    gi_ref[...] = dot_tn(normed_ref[...], gproj_ref[:, : 2 * part])
    if slots == 0:
        send_ref[...] = gi_ref[...].astype(BF16)
        keep_ref[...] = jnp.zeros_like(keep_ref)
    else:
        block = width // groups
        rows = block // slots
        for s in range(slots):
            parts = [slot_rows(gi_ref, block, rows, me, pos, t, s) for t in range(groups)]
            both = jnp.concatenate(parts, axis=0).astype(BF16)
            if s % 2:
                send_ref[s // 2] = both
            else:
                keep_ref[s // 2] = both
    gn_ref[...] = dot_nt(gproj_ref[...], wfull_ref[...])
    total = jnp.zeros((1, width), F32)
    for k in range(groups):
        x = tok[k][...].astype(F32)
        gn = gn_ref[rows_at(me ^ k, count), :]
        total = total + jnp.sum(gn * (x * norm_scale(x)), axis=0, keepdims=True)
        if k == 0:
            own_ref[...] = gn
        elif k == 2:
            mid_ref[...] = gn
        elif k == 1:
            rows_ref[0:count, :] = gn.astype(BF16)
        else:
            rows_ref[count : 2 * count, :] = gn.astype(BF16)
    small_ref[...] = early_ref[...]
    small_ref[12:13, :] = total
    for h in range(heads):
        tile, rest = tiles[h]
        far = jnp.sum(rest, axis=0, keepdims=True)
        far = jnp.concatenate([far, jnp.zeros_like(far)], axis=1)
        sums = []
        for n in range(NB):
            inside = distance >= STARTS[n]
            if n + 1 < NB:
                inside = inside & (distance < STARTS[n + 1])
            one = jnp.sum(jnp.where(inside, tile, 0.0), axis=0, keepdims=True)
            sums.append(one + far if n == NB - 1 else one)
        sums = jnp.transpose(jnp.concatenate(sums, axis=0))
        line = jnp.sum(sums, axis=0, keepdims=True)
        index = lax.broadcasted_iota(jnp.int32, (16, NB), 0)
        small_ref[0:16, 0:NB] += jnp.where(index == me * heads + h, line, 0.0)


def natural(pieces, me):
    out = []
    for w in range(len(pieces)):
        value = pieces[0]
        for t in range(1, len(pieces)):
            value = jnp.where((me ^ w) == t, pieces[t], value)
        out.append(value)
    return jnp.concatenate(out, axis=1)


def join_kernel(groups, me_ref, *refs):
    pieces = [r[...].astype(F32) for r in refs[:groups]]
    rest = refs[groups:-1]
    me = me_ref[0]
    if rest:
        both = [rest[0][...].astype(F32), natural(pieces, me)]
    else:
        half = pieces[0].shape[1] // 2
        both = [natural([p[:, i * half : (i + 1) * half] for p in pieces], me) for i in range(2)]
    refs[-1][...] = jnp.concatenate(both, axis=0).astype(BF16)


def final_kernel(slots, me_ref, *refs):
    first = refs[0:2]
    second = refs[2:4]
    out_ref, own_ref = refs[4:]
    pos = me_ref[1]
    rows = out_ref.shape[0] // slots
    third = out_ref.shape[1] // 3
    for s in range(slots):
        target = pl.ds(pl.multiple_of((pos ^ s) * rows, 8), rows)
        one = first[s % 2][s // 2].astype(F32)
        two = second[s % 2][s // 2].astype(F32)
        own_ref[target, :] = one[:rows]
        out_ref[target, 2 * third :] = one[rows:]
        out_ref[target, :third] = two[:rows]
        out_ref[target, third : 2 * third] = two[rows:]


def reduce_slots(send, keep, axis):
    bit = 1
    while True:
        got = exchange(send, axis, bit)
        total = keep.astype(F32) + got.astype(F32)
        if total.shape[0] == 1:
            return total[0]
        send = total[1::2].astype(BF16)
        keep = total[0::2].astype(BF16)
        bit *= 2


def spread_slots(value, axis):
    bit = lax.axis_size(axis) // 2
    while True:
        got = exchange(value, axis, bit)
        if bit == 1:
            return value, got
        value = jnp.stack([value, got], axis=1).reshape((-1,) + value.shape[1:])
        bit //= 2


def sum_all(value, axes):
    for axis in axes:
        bit = 1
        while bit < lax.axis_size(axis):
            sent = value.astype(BF16)
            value = sent.astype(F32) + exchange(sent, axis, bit).astype(F32)
            bit *= 2
    return value


def reduce_rows(send, keep, mid, axis):
    rows = keep.shape[0]
    got = exchange(send, axis, 1).astype(F32)
    other = (mid + got[rows:]).astype(BF16)
    return keep + got[:rows] + exchange(other, axis, 2).astype(F32)


def body(
    tokens,
    gain_attention,
    gain_experts,
    proj_inputs,
    proj_output,
    bias_table,
    router_weight,
    routes,
    slot_index,
    drop_flags,
    expert_in,
    expert_out,
    cotangent,
):
    groups = lax.axis_size("wshard")
    size = lax.axis_size("expert")
    me = lax.axis_index("wshard")
    pos = lax.axis_index("expert")
    where = jnp.stack([me, pos]).astype(jnp.int32)
    count, width = tokens.shape
    length = count * groups
    heads_all = bias_table.shape[1]
    heads = heads_all // groups
    hs = width // heads_all
    part = width // groups
    local = expert_in.shape[0]
    experts = local * size
    hidden_local = expert_in.shape[2]
    buckets = bias_table.shape[0] * groups

    table = jnp.concatenate(
        [routes.T, slot_index.T, drop_flags.T, jnp.zeros((2, count), jnp.int32)], axis=0
    ).astype(F32)

    extra_rows = 16 + experts
    small = jnp.zeros((extra_rows, width), BF16)
    small = lax.dynamic_update_slice(small, bias_table.T, (0, me * bias_table.shape[0]))
    small = lax.dynamic_update_slice(
        small, jnp.stack([gain_attention, gain_experts]), (12, me * part)
    )
    small = lax.dynamic_update_slice(small, router_weight.T, (16, me * part))

    tok = gather_xor(tokens, "wshard")
    chunks = whole(
        lambda *r: prepare_kernel(groups, *r),
        [((part, 3 * part), BF16)] * groups,
        where,
        proj_inputs,
        scratch=[pltpu.VMEM((groups, part, 3 * part), BF16)],
    )
    wp = [chunks[0]] + [exchange(chunks[k], "wshard", k) for k in range(1, groups)]
    ext = gather_xor(small, "wshard")
    wo = gather_xor(proj_output, "wshard")

    front = whole(
        lambda *r: front_kernel(groups, heads, hs, *r),
        [
            ((length, width), BF16),
            ((width, 3 * part), BF16),
            ((length, 3 * part), BF16),
            ((length, part), BF16),
            ((heads, length, length), F32),
        ]
        + [((count, part), BF16)] * groups,
        where,
        *tok,
        *wp,
        *ext,
        scratch=[pltpu.VMEM((extra_rows, width), F32)],
    )
    normed_one, wfull, projected, mixed, prob = front[:5]
    mine = front[5:]
    pieces = [mine[0]] + [exchange(mine[k], "wshard", k) for k in range(1, groups)]

    slots = experts * CAP
    residual, normed_two, send, gates = whole(
        lambda *r: middle_kernel(groups, experts, *r),
        [
            ((count, width), F32),
            ((count, width), BF16),
            ((slots, 2 * width), BF16),
            ((count, 128), F32),
        ],
        *pieces,
        *wo,
        *ext,
        tokens,
        cotangent,
        table,
        smem=0,
    )
    sent = lax.all_to_all(
        send.reshape(size, local * CAP, 2 * width), "expert", 0, 0, tiled=True
    ).reshape(slots, 2 * width)
    xs = gather_xor(sent, "wshard")

    rows = slots * groups
    fblock = 256
    steps = hidden_local // fblock
    full = pl.BlockSpec((slots, 2 * width), lambda f: (0, 0))
    hidden, gpre, back_send, back_keep, back_mid = pl.pallas_call(
        lambda *r: experts_kernel(groups, local, *r),
        grid=(steps,),
        in_specs=[full] * groups
        + [
            pl.BlockSpec((local, width, fblock), lambda f: (0, 0, f)),
            pl.BlockSpec((local, fblock, width), lambda f: (0, f, 0)),
        ],
        out_specs=[
            pl.BlockSpec((rows, fblock), lambda f: (0, f)),
            pl.BlockSpec((rows, fblock), lambda f: (0, f)),
            pl.BlockSpec((2 * slots, 2 * width), lambda f: (0, 0)),
            pl.BlockSpec((slots, 2 * width), lambda f: (0, 0)),
            pl.BlockSpec((slots, 2 * width), lambda f: (0, 0)),
        ],
        out_shape=[
            jax.ShapeDtypeStruct((rows, hidden_local), BF16),
            jax.ShapeDtypeStruct((rows, hidden_local), BF16),
            jax.ShapeDtypeStruct((2 * slots, 2 * width), BF16),
            jax.ShapeDtypeStruct((slots, 2 * width), F32),
            jax.ShapeDtypeStruct((slots, 2 * width), F32),
        ],
        scratch_shapes=[
            pltpu.VMEM((rows, 2 * width), BF16),
            pltpu.VMEM((rows, 2 * width), F32),
        ],
    )(*xs, expert_in, expert_out)

    full2 = pl.BlockSpec((slots, 2 * width), lambda j, f: (0, 0))
    weights_call = pl.pallas_call(
        lambda *r: weights_kernel(groups, local, *r),
        grid=(local, steps),
        in_specs=[full2] * groups
        + [
            pl.BlockSpec((rows, fblock), lambda j, f: (0, f)),
            pl.BlockSpec((rows, fblock), lambda j, f: (0, f)),
        ],
        out_specs=[
            pl.BlockSpec((1, width, fblock), lambda j, f: (j, 0, f)),
            pl.BlockSpec((1, fblock, width), lambda j, f: (j, f, 0)),
        ],
        out_shape=[
            jax.ShapeDtypeStruct(expert_in.shape, F32),
            jax.ShapeDtypeStruct(expert_out.shape, F32),
        ],
        scratch_shapes=[pltpu.VMEM((rows, 2 * width), BF16)],
    )
    grad_expert_in, grad_expert_out = weights_call(*xs, hidden, gpre)

    returned = reduce_rows(back_send, back_keep, back_mid, "wshard").astype(BF16)
    returned = lax.all_to_all(
        returned.reshape(size, local * CAP, 2 * width), "expert", 0, 0, tiled=True
    ).reshape(slots, 2 * width)

    output, grad_residual, grad_res_b, early = whole(
        lambda *r: return_kernel(groups, experts, *r),
        [
            ((count, width), BF16),
            ((count, width), F32),
            ((count, width), BF16),
            ((experts + 16, width), F32),
        ],
        *ext,
        returned,
        residual,
        normed_two,
        gates,
        cotangent,
        table,
        smem=0,
    )
    gr = gather_xor(grad_res_b, "wshard")
    fast = part % (8 * size) == 0
    cuts = size if fast else 0
    step = part // size
    first_shapes = [((part, width), BF16), ((width, part), BF16)]
    second_shapes = [((width, 2 * part), BF16), ((8, 128), BF16)]
    if fast:
        first_shapes = [((size // 2, 2 * step, width), BF16)] * 2
        second_shapes = [((size // 2, groups * step, 2 * part), BF16)] * 2
    gm, gv, first_send, first_keep = whole(
        lambda *r: values_kernel(groups, heads, hs, cuts, *r),
        [((length, part), BF16), ((length, part), BF16)] + first_shapes,
        where,
        *gr,
        proj_output,
        mixed,
        prob,
        normed_one,
        scratch=[
            pltpu.VMEM((length, width), BF16),
            pltpu.VMEM((part, width), F32),
            pltpu.VMEM((width, part), F32),
        ],
    )
    second_send, second_keep, gn_send, gn_keep, gn_mid, sums = whole(
        lambda *r: scores_kernel(groups, heads, hs, cuts, *r),
        second_shapes
        + [
            ((2 * count, width), BF16),
            ((count, width), F32),
            ((count, width), F32),
            ((experts + 16, width), F32),
        ],
        where,
        *tok,
        gm,
        gv,
        projected,
        prob,
        normed_one,
        wfull,
        early,
        scratch=[
            pltpu.VMEM((length, 3 * part), BF16),
            pltpu.VMEM((width, 2 * part), F32),
            pltpu.VMEM((length, width), F32),
        ],
    )
    grad_normed_one = reduce_rows(gn_send, gn_keep, gn_mid, "wshard")
    inputs = tokens.astype(F32)
    scale_one = norm_scale(inputs)
    gain_one_f = sum(e[12:13].astype(F32) for e in ext)
    scaled = grad_normed_one * gain_one_f
    inner = jnp.mean(scaled * inputs, axis=-1, keepdims=True)
    grad_tokens = grad_residual + (
        scale_one * scaled - inputs * scale_one * scale_one * scale_one * inner
    )

    sums = sum_all(sums, ("wshard", "expert"))
    grad_router = lax.dynamic_slice(sums[16:], (0, me * part), (experts, part)).T
    grad_gain_two = lax.dynamic_slice(sums[13], (me * part,), (part,))
    grad_gain_one = lax.dynamic_slice(sums[12], (me * part,), (part,))
    per = buckets // groups
    grad_table = lax.dynamic_slice(sums, (0, me * per), (heads_all, per)).T

    if fast:
        one = reduce_slots(first_send, first_keep, "expert").astype(BF16)
        cut = [one[step:, t * part : (t + 1) * part] for t in range(groups)]
        cut = [cut[0]] + [exchange(cut[t], "wshard", t) for t in range(1, groups)]
        one = whole(
            lambda *r: join_kernel(groups, *r),
            [((2 * step, width), BF16)],
            where,
            *cut,
            one[:step],
        )[0]
        one = spread_slots(one[None], "expert")
        two = reduce_slots(second_send, second_keep, "expert").astype(BF16)
        cut = [two[t * step : (t + 1) * step] for t in range(groups)]
        cut = [cut[0]] + [exchange(cut[t], "wshard", t) for t in range(1, groups)]
        two = whole(
            lambda *r: join_kernel(groups, *r), [((2 * step, width), BF16)], where, *cut
        )[0]
        two = spread_slots(two[None], "expert")
        total_inputs, total_output = whole(
            lambda *r: final_kernel(size, *r),
            [((part, 3 * width), F32), ((part, width), F32)],
            where,
            *one,
            *two,
        )
    else:
        total_output = lax.psum(first_send.astype(F32), "expert")
        total = jnp.concatenate([second_send, first_keep], axis=1)
        total = lax.psum(total, "expert").reshape(groups, part, 3, part)
        total = lax.all_to_all(total, "wshard", 0, 0, tiled=True)
        total_inputs = total.transpose(1, 2, 0, 3).reshape(part, 3 * width).astype(F32)
    return (
        output,
        grad_tokens,
        grad_gain_one,
        grad_gain_two,
        total_inputs,
        total_output,
        grad_table,
        grad_router,
        grad_expert_in,
        grad_expert_out,
    )


def solution(mesh):
    placed = (
        P(("expert", "wshard"), None),
        P("wshard"),
        P("wshard"),
        P("wshard", None),
        P("wshard", None),
        P("wshard", None),
        P("wshard", None),
        P(("expert", "wshard"), None),
        P(("expert", "wshard"), None),
        P(("expert", "wshard"), None),
        P("expert", None, "wshard"),
        P("expert", "wshard", None),
        P(("expert", "wshard"), None),
    )
    return jax.shard_map(
        body,
        mesh=mesh,
        in_specs=placed,
        out_specs=(
            P(("expert", "wshard"), None),
            P(("expert", "wshard"), None),
            P("wshard"),
            P("wshard"),
            P("wshard", None),
            P("wshard", None),
            P("wshard", None),
            P("wshard", None),
            P("expert", None, "wshard"),
            P("expert", "wshard", None),
        ),
        check_vma=False,
    )
```

```python
import math

import jax
import jax.numpy as jnp
from jax import lax
from jax.experimental import pallas as pl
from jax.experimental.pallas import tpu as pltpu
from jax.sharding import PartitionSpec as P


NB = 32
MAXDIST = 128
CAP = 4
EPSILON = 1e-06
NEGATIVE = -1e30
BLOCK = 128
F32 = jnp.float32
BF16 = jnp.bfloat16


def bucket_starts():
    exact = NB // 2
    starts = list(range(exact + 1))
    for level in range(1, exact):
        starts.append(math.ceil(exact * (MAXDIST / exact) ** (level / exact) - 1e-09))
    return starts


STARTS = bucket_starts()


def exchange(value, axis, mask):
    size = lax.axis_size(axis)
    return lax.ppermute(value, axis, [(i, i ^ mask) for i in range(size)])


def gather_xor(value, axis):
    pieces = {0: value}
    bit = lax.axis_size(axis) // 2
    while bit >= 1:
        for key in list(pieces):
            pieces[key | bit] = exchange(pieces[key], axis, bit)
        bit //= 2
    return [pieces[k] for k in range(len(pieces))]


def whole(kernel, outs, *args, scratch=(), smem=1):
    return call_whole(kernel, outs, *args, scratch=scratch, smem=smem)


def call_whole(kernel, outs, *args, scratch, smem):
    specs = [pl.BlockSpec(memory_space=pltpu.SMEM)] * smem
    specs += [pl.BlockSpec(memory_space=pltpu.VMEM)] * (len(args) - smem)
    return pl.pallas_call(
        kernel,
        out_shape=[jax.ShapeDtypeStruct(s, d) for s, d in outs],
        in_specs=specs,
        out_specs=[pl.BlockSpec(memory_space=pltpu.VMEM)] * len(outs),
        scratch_shapes=list(scratch),
    )(*args)


def dot_nn(a, b):
    return lax.dot_general(a, b, (((1,), (0,)), ((), ())), preferred_element_type=F32)


def dot_nt(a, b):
    return lax.dot_general(a, b, (((1,), (1,)), ((), ())), preferred_element_type=F32)


def dot_tn(a, b):
    return lax.dot_general(a, b, (((0,), (0,)), ((), ())), preferred_element_type=F32)


def norm_scale(values):
    return lax.rsqrt(jnp.mean(values * values, axis=-1, keepdims=True) + EPSILON)


def sum_refs(refs):
    total = refs[0][...].astype(F32)
    for ref in refs[1:]:
        total = total + ref[...].astype(F32)
    return total


def distance_tile():
    rows = lax.broadcasted_iota(jnp.int32, (BLOCK, 2 * BLOCK), 0)
    cols = lax.broadcasted_iota(jnp.int32, (BLOCK, 2 * BLOCK), 1)
    return rows + BLOCK - cols


def rows_at(index, size):
    return pl.ds(pl.multiple_of(index * size, size & -size), size)


def prepare_kernel(groups, me_ref, w_ref, *outs_and_scratch):
    outs = outs_and_scratch[:groups]
    chunks = outs_and_scratch[groups]
    me = me_ref[0]
    third = w_ref.shape[1] // 3
    part = third // groups
    for d in range(groups):
        for s in range(2):
            chunks[d, 0:part, s * part : (s + 1) * part] = w_ref[
                :, s * third + d * part : s * third + (d + 1) * part
            ]
        for s in range(2):
            chunks[d, part:, s * part : (s + 1) * part] = w_ref[
                s * part // 2 : (s + 1) * part // 2, 2 * third + d * part : 2 * third + (d + 1) * part
            ]
    for k in range(groups):
        outs[k][...] = chunks[me ^ k]


def score_blocks(q, k, tile, far, qb, factor):
    blocks = []
    for kb in range(qb + 1):
        s = dot_nt(q, k[kb * BLOCK : (kb + 1) * BLOCK]) * factor
        if kb == qb:
            s = s + tile[:, BLOCK:]
        elif kb == qb - 1:
            s = s + tile[:, :BLOCK]
        else:
            s = s + far
        blocks.append(s)
    return blocks


def front_kernel(groups, heads, hs, me_ref, *refs):
    tok = refs[:groups]
    wp = refs[groups : 2 * groups]
    ext = refs[2 * groups : 3 * groups]
    outs = refs[3 * groups :]
    normed_ref, wfull_ref, proj_ref, mixed_ref, prob_ref = outs[:5]
    pieces = outs[5 : 5 + groups]
    tab_ref = outs[5 + groups]
    me = me_ref[0]
    count = tok[0].shape[0]
    wrows = wp[0].shape[0] * 2 // 3
    length = count * groups
    extra = sum_refs(ext)
    gain = extra[12:13, :]
    tab_ref[...] = extra
    for k in range(groups):
        x = tok[k][...].astype(F32)
        normed_ref[rows_at(me ^ k, count), :] = (x * norm_scale(x) * gain).astype(BF16)
        cols = 2 * heads * hs
        wfull_ref[rows_at(me ^ k, wrows), :cols] = wp[k][:wrows, :]
        for s in range(2):
            wfull_ref[rows_at(2 * (me ^ k) + s, wrows // 2), cols:] = wp[k][
                wrows:, s * cols // 2 : (s + 1) * cols // 2
            ]
    proj_ref[...] = dot_nn(normed_ref[...], wfull_ref[...]).astype(BF16)
    distance = distance_tile()
    factor = hs ** (-0.5)
    part = heads * hs
    tiles = []
    fars = []
    for h in range(heads):
        row = tab_ref[pl.ds(me * heads + h, 1), :]
        tile = jnp.broadcast_to(row[:, 0:1], distance.shape)
        for n in range(1, NB):
            tile = jnp.where(distance >= STARTS[n], row[:, n : n + 1], tile)
        tiles.append(jnp.where(distance >= 0, tile, NEGATIVE))
        fars.append(row[:, NB - 1 : NB])
    for qb in range(length // BLOCK):
        span = slice(qb * BLOCK, (qb + 1) * BLOCK)
        keys = (qb + 1) * BLOCK
        mixed = []
        for h in range(heads):
            q = proj_ref[span, h * hs : (h + 1) * hs]
            k = proj_ref[:keys, part + h * hs : part + (h + 1) * hs]
            v = proj_ref[:keys, 2 * part + h * hs : 2 * part + (h + 1) * hs]
            blocks = score_blocks(q, k, tiles[h], fars[h], qb, factor)
            top = blocks[0]
            for s in blocks[1:]:
                top = jnp.maximum(top, s)
            top = jnp.max(top, axis=-1, keepdims=True)
            es = [jnp.exp(s - top) for s in blocks]
            total = es[0]
            for e in es[1:]:
                total = total + e
            total = jnp.sum(total, axis=-1, keepdims=True)
            inverse = 1.0 / total
            w = jnp.concatenate([e * inverse for e in es], axis=1)
            prob_ref[h, span, :keys] = w
            mixed.append(dot_nn(w.astype(BF16), v))
        mixed_ref[span, :] = jnp.concatenate(mixed, axis=1).astype(BF16)
    for k in range(groups):
        pieces[k][...] = mixed_ref[rows_at(me ^ k, count), :]


def columns(table_ref):
    table = jnp.transpose(table_ref[...])
    return [table[:, i : i + 1] for i in range(6)]


def places_of(cols, slots):
    ids = lax.broadcasted_iota(jnp.int32, (cols[0].shape[0], slots), 1).astype(F32)
    flat = [cols[r] * float(CAP) + cols[2 + r] for r in range(2)]
    flat = [jnp.where(cols[4 + r] == 0.0, flat[r], -1.0) for r in range(2)]
    return [(f == ids).astype(F32).astype(BF16) for f in flat]


def route_onehot(cols, experts):
    ids = lax.broadcasted_iota(jnp.int32, (cols[0].shape[0], experts), 1).astype(F32)
    return [(cols[r] == ids).astype(F32) for r in range(2)]


def middle_kernel(groups, experts, *refs):
    mixed = refs[:groups]
    wo = refs[groups : 2 * groups]
    ext = refs[2 * groups : 3 * groups]
    tok_ref, cot_ref, table_ref = refs[3 * groups : 3 * groups + 3]
    residual_ref, normed_ref, send_ref, gates_ref = refs[3 * groups + 3 :]
    cols = columns(table_ref)
    count, width = tok_ref.shape
    total = dot_nn(mixed[0][...], wo[0][...])
    for k in range(1, groups):
        total = total + dot_nn(mixed[k][...], wo[k][...])
    residual = tok_ref[...].astype(F32) + total
    residual_ref[...] = residual
    extra = sum_refs(ext)
    gain = extra[13:14, :]
    router = extra[16 : 16 + experts, :].astype(BF16)
    normed = (residual * norm_scale(residual) * gain).astype(BF16)
    normed_ref[...] = normed
    logits = dot_nt(normed, router)
    onehot = route_onehot(cols, experts)
    chosen = [jnp.sum(logits * o, axis=1, keepdims=True) for o in onehot]
    top = jnp.maximum(chosen[0], chosen[1])
    ex = [jnp.exp(c - top) for c in chosen]
    both = ex[0] + ex[1]
    gates = [e / both for e in ex]
    keep = [1.0 - cols[4], 1.0 - cols[5]]
    places = places_of(cols, experts * CAP)
    up = cot_ref[...].astype(F32)
    send_ref[:, :width] = dot_tn(places[0] + places[1], normed).astype(BF16)
    grads = dot_tn(places[0], (gates[0] * keep[0] * up).astype(BF16))
    grads = grads + dot_tn(places[1], (gates[1] * keep[1] * up).astype(BF16))
    send_ref[:, width:] = grads.astype(BF16)
    lanes = lax.broadcasted_iota(jnp.int32, (count, 128), 1)
    gates_ref[...] = jnp.where(lanes == 0, gates[0], gates[1])


def owner_mask(rows, local, j):
    index = lax.broadcasted_iota(jnp.int32, (rows, 1), 0)
    return (index // CAP) % local == j


def experts_kernel(groups, local, *refs):
    xs = refs[:groups]
    win_ref, wout_ref = refs[groups : groups + 2]
    hidden_ref, gpre_ref, send_ref, keep_ref, mid_ref, x_ref, acc_ref = refs[groups + 2 :]
    step = pl.program_id(0)
    rows = xs[0].shape[0]
    width = xs[0].shape[1] // 2

    @pl.when(step == 0)
    def _():
        for k in range(groups):
            x_ref[k * rows : (k + 1) * rows, :] = xs[k][...]
        acc_ref[...] = jnp.zeros_like(acc_ref)

    r = x_ref[:, :width]
    g = x_ref[:, width:]
    masks = [owner_mask(rows * groups, local, j) for j in range(local)]
    pre = dot_nn(r, win_ref[0])
    gh = dot_nt(g, wout_ref[0])
    for j in range(1, local):
        pre = jnp.where(masks[j], dot_nn(r, win_ref[j]), pre)
        gh = jnp.where(masks[j], dot_nt(g, wout_ref[j]), gh)
    root = math.sqrt(2.0 / math.pi)
    square = pre * pre
    th = jnp.tanh(root * (pre + 0.044715 * (square * pre)))
    cdf = 0.5 * (1.0 + th)
    hid = pre * cdf
    slope = cdf + 0.5 * pre * (1.0 - th * th) * (root * (1.0 + 3.0 * 0.044715 * square))
    gp = gh * slope
    hidden_ref[...] = hid.astype(BF16)
    gpre_ref[...] = gp.astype(BF16)
    for j in range(local):
        acc_ref[:, :width] += dot_nn(jnp.where(masks[j], hid, 0.0).astype(BF16), wout_ref[j])
        acc_ref[:, width:] += dot_nt(jnp.where(masks[j], gp, 0.0).astype(BF16), win_ref[j])

    @pl.when(step == pl.num_programs(0) - 1)
    def _():
        keep_ref[...] = acc_ref[0:rows, :]
        mid_ref[...] = acc_ref[2 * rows : 3 * rows, :]
        send_ref[0:rows, :] = acc_ref[rows : 2 * rows, :].astype(BF16)
        send_ref[rows : 2 * rows, :] = acc_ref[3 * rows : 4 * rows, :].astype(BF16)


def weights_kernel(groups, local, *refs):
    xs = refs[:groups]
    hidden_ref, gpre_ref, gin_ref, gout_ref, x_ref = refs[groups:]
    j = pl.program_id(0)
    rows = xs[0].shape[0]
    width = xs[0].shape[1] // 2

    @pl.when(pl.program_id(1) == 0)
    def _():
        for k in range(groups):
            x_ref[k * rows : (k + 1) * rows, :] = xs[k][...]

    mask = owner_mask(rows * groups, local, j)
    gp = jnp.where(mask, gpre_ref[...].astype(F32), 0.0).astype(BF16)
    hid = jnp.where(mask, hidden_ref[...].astype(F32), 0.0).astype(BF16)
    gin_ref[0] = dot_tn(x_ref[:, :width], gp)
    gout_ref[0] = dot_tn(hid, x_ref[:, width:])


def return_kernel(groups, experts, *refs):
    ext = refs[:groups]
    back_ref, residual_ref, normed_ref, gates_ref, cot_ref = refs[groups : groups + 5]
    table_ref = refs[groups + 5]
    out_ref, gres_ref, gresb_ref, small_ref = refs[groups + 6 :]
    cols = columns(table_ref)
    _, width = cot_ref.shape
    places = places_of(cols, experts * CAP)
    onehot = route_onehot(cols, experts)
    keep = [1.0 - cols[4], 1.0 - cols[5]]
    gates = [gates_ref[:, 0:1], gates_ref[:, 1:2]]
    up = cot_ref[...].astype(F32)
    residual = residual_ref[...]
    values = back_ref[:, :width]
    picked = [dot_nn(p, values) for p in places]
    moe = gates[0] * keep[0] * picked[0] + gates[1] * keep[1] * picked[1]
    out_ref[...] = (residual + moe).astype(BF16)
    gg = [keep[r] * jnp.sum(up * picked[r], axis=1, keepdims=True) for r in range(2)]
    mean = gates[0] * gg[0] + gates[1] * gg[1]
    gc = [gates[r] * (gg[r] - mean) for r in range(2)]
    glog = (onehot[0] * gc[0] + onehot[1] * gc[1]).astype(BF16)
    extra = sum_refs(ext)
    gain = extra[13:14, :]
    router = extra[16 : 16 + experts, :].astype(BF16)
    gn = dot_nn(places[0] + places[1], back_ref[:, width:]) + dot_nn(glog, router)
    scale = norm_scale(residual)
    small_ref[0:16, :] = jnp.zeros((16, width), F32)
    small_ref[13:14, :] = jnp.sum(gn * residual * scale, axis=0, keepdims=True)
    small_ref[16 : 16 + experts, :] = dot_tn(glog, normed_ref[...])
    scaled = gn * gain
    inner = jnp.mean(scaled * residual, axis=-1, keepdims=True)
    gres = up + scale * scaled - residual * (scale * scale * scale * inner)
    gres_ref[...] = gres
    gresb_ref[...] = gres.astype(BF16)


def slot_rows(ref, block, rows, me, pos, t, s):
    return ref[pl.ds(pl.multiple_of((me ^ t) * block + (pos ^ s) * rows, 8), rows), :]


def values_kernel(groups, heads, hs, slots, me_ref, *refs):
    gr = refs[:groups]
    wo_ref, mixed_ref, prob_ref, normed_ref = refs[groups : groups + 4]
    gm_ref, gv_ref, send_ref, keep_ref, grf_ref, go_ref, gi_ref = refs[groups + 4 :]
    me = me_ref[0]
    pos = me_ref[1]
    count = gr[0].shape[0]
    length = count * groups
    for k in range(groups):
        grf_ref[rows_at(me ^ k, count), :] = gr[k][...]
    gm_ref[...] = dot_nt(grf_ref[...], wo_ref[...]).astype(BF16)
    go_ref[...] = dot_tn(mixed_ref[...], grf_ref[...])
    for b in range(length // BLOCK):
        cut = slice(b * BLOCK, (b + 1) * BLOCK)
        dv = [
            dot_tn(
                prob_ref[h, b * BLOCK :, cut].astype(BF16),
                gm_ref[b * BLOCK :, h * hs : (h + 1) * hs],
            )
            for h in range(heads)
        ]
        gv_ref[cut, :] = jnp.concatenate(dv, axis=1).astype(BF16)
    gi_ref[...] = dot_tn(normed_ref[...], gv_ref[...])
    if slots == 0:
        send_ref[...] = go_ref[...].astype(BF16)
        keep_ref[...] = gi_ref[...].astype(BF16)
        return
    block = go_ref.shape[0]
    rows = block // slots
    for s in range(slots):
        own = go_ref[pl.ds(pl.multiple_of((pos ^ s) * rows, 8), rows), :]
        parts = [slot_rows(gi_ref, block, rows, me, pos, t, s) for t in range(groups)]
        both = jnp.concatenate([own, jnp.concatenate(parts, axis=1)], axis=0).astype(BF16)
        if s % 2:
            send_ref[s // 2] = both
        else:
            keep_ref[s // 2] = both


def scores_kernel(groups, heads, hs, slots, me_ref, *refs):
    gm_ref, gv_ref, proj_ref, prob_ref, normed_ref = refs[:5]
    send_ref, keep_ref, gproj_ref, tiles_ref, gi_ref = refs[5:]
    me = me_ref[0]
    pos = me_ref[1]
    length, width = normed_ref.shape
    factor = hs ** (-0.5)
    part = heads * hs
    blocks_n = length // BLOCK
    dqs = [[None] * heads for _ in range(blocks_n)]
    dks = [[None] * heads for _ in range(blocks_n)]
    for h in range(heads):
        near = jnp.zeros((BLOCK, BLOCK), F32)
        prev = jnp.zeros((BLOCK, BLOCK), F32)
        rest = jnp.zeros((BLOCK, BLOCK), F32)
        for qb in range(blocks_n):
            span = slice(qb * BLOCK, (qb + 1) * BLOCK)
            keys = (qb + 1) * BLOCK
            q = proj_ref[span, h * hs : (h + 1) * hs]
            k = proj_ref[:keys, part + h * hs : part + (h + 1) * hs]
            v = proj_ref[:keys, 2 * part + h * hs : 2 * part + (h + 1) * hs]
            gm = gm_ref[span, h * hs : (h + 1) * hs]
            p = prob_ref[h, span, :keys]
            gw = dot_nt(gm, v)
            inner = jnp.sum(p * gw, axis=-1, keepdims=True)
            ds = p * (gw - inner)
            near = near + ds[:, qb * BLOCK :]
            if qb >= 1:
                prev = prev + ds[:, (qb - 1) * BLOCK : qb * BLOCK]
            for kb in range(qb - 1):
                rest = rest + ds[:, kb * BLOCK : (kb + 1) * BLOCK]
            dsb = ds.astype(BF16)
            dqs[qb][h] = dot_nn(dsb, k) * factor
            dk = dot_tn(dsb, q)
            for kb in range(qb + 1):
                cut = slice(kb * BLOCK, (kb + 1) * BLOCK)
                if dks[kb][h] is None:
                    dks[kb][h] = dk[cut]
                else:
                    dks[kb][h] = dks[kb][h] + dk[cut]
        tiles_ref[h] = jnp.concatenate([prev, near, rest], axis=1)
    for b in range(blocks_n):
        span = slice(b * BLOCK, (b + 1) * BLOCK)
        full = jnp.concatenate(dqs[b] + [d * factor for d in dks[b]], axis=1)
        gproj_ref[span, : 2 * part] = full.astype(BF16)
    gproj_ref[:, 2 * part :] = gv_ref[...]
    gi_ref[...] = dot_tn(normed_ref[...], gproj_ref[:, : 2 * part])
    if slots == 0:
        send_ref[...] = gi_ref[...].astype(BF16)
        keep_ref[...] = jnp.zeros_like(keep_ref)
    else:
        block = width // groups
        rows = block // slots
        for s in range(slots):
            parts = [slot_rows(gi_ref, block, rows, me, pos, t, s) for t in range(groups)]
            both = jnp.concatenate(parts, axis=0).astype(BF16)
            if s % 2:
                send_ref[s // 2] = both
            else:
                keep_ref[s // 2] = both


def rest_kernel(groups, heads, me_ref, *refs):
    tok = refs[:groups]
    gproj_ref, wfull_ref, tiles_ref, early_ref = refs[groups : groups + 4]
    rows_ref, own_ref, mid_ref, small_ref, gn_ref = refs[groups + 4 :]
    me = me_ref[0]
    count, width = tok[0].shape
    distance = distance_tile()
    gn_ref[...] = dot_nt(gproj_ref[...], wfull_ref[...])
    total = jnp.zeros((1, width), F32)
    for k in range(groups):
        x = tok[k][...].astype(F32)
        gn = gn_ref[rows_at(me ^ k, count), :]
        total = total + jnp.sum(gn * (x * norm_scale(x)), axis=0, keepdims=True)
        if k == 0:
            own_ref[...] = gn
        elif k == 2:
            mid_ref[...] = gn
        elif k == 1:
            rows_ref[0:count, :] = gn.astype(BF16)
        else:
            rows_ref[count : 2 * count, :] = gn.astype(BF16)
    small_ref[...] = early_ref[...]
    small_ref[12:13, :] = total
    for h in range(heads):
        tile = tiles_ref[h, :, : 2 * BLOCK]
        far = jnp.sum(tiles_ref[h, :, 2 * BLOCK :], axis=0, keepdims=True)
        far = jnp.concatenate([far, jnp.zeros_like(far)], axis=1)
        sums = []
        for n in range(NB):
            inside = distance >= STARTS[n]
            if n + 1 < NB:
                inside = inside & (distance < STARTS[n + 1])
            one = jnp.sum(jnp.where(inside, tile, 0.0), axis=0, keepdims=True)
            sums.append(one + far if n == NB - 1 else one)
        sums = jnp.transpose(jnp.concatenate(sums, axis=0))
        line = jnp.sum(sums, axis=0, keepdims=True)
        index = lax.broadcasted_iota(jnp.int32, (16, NB), 0)
        placed = jnp.where(index == me * heads + h, line, 0.0)
        per = NB // groups
        for w in range(groups):
            at = w * (width // groups)
            small_ref[0:16, at : at + per] += placed[:, w * per : (w + 1) * per]
    rows_ref[2 * count :, :] = small_ref[...].astype(BF16)


def natural(pieces, me):
    out = []
    for w in range(len(pieces)):
        value = pieces[0]
        for t in range(1, len(pieces)):
            value = jnp.where((me ^ w) == t, pieces[t], value)
        out.append(value)
    return jnp.concatenate(out, axis=1)


def join_kernel(groups, me_ref, *refs):
    pieces = [r[...].astype(F32) for r in refs[:groups]]
    own_ref, rider_ref, first_ref, second_ref = refs[groups:]
    me = me_ref[0]
    part = pieces[0].shape[1] // 3
    q, k, v = [natural([p[:, i * part : (i + 1) * part] for p in pieces], me) for i in range(3)]
    first = jnp.concatenate([own_ref[...].astype(F32), v, rider_ref[...]], axis=0)
    first_ref[...] = first.astype(BF16)
    second_ref[...] = jnp.concatenate([q, k], axis=0).astype(BF16)


def final_kernel(slots, me_ref, *refs):
    first = refs[0:2]
    second = refs[2:4]
    out_ref, own_ref = refs[4:]
    pos = me_ref[1]
    rows = out_ref.shape[0] // slots
    third = out_ref.shape[1] // 3
    for s in range(slots):
        target = pl.ds(pl.multiple_of((pos ^ s) * rows, 8), rows)
        at = [spread_place(s, spread_bits(slots, swap)) * 2 * rows for swap in (False, True)]
        one = first[s % 2][at[0] : at[0] + 2 * rows, :].astype(F32)
        two = second[s % 2][at[1] : at[1] + 2 * rows, :].astype(F32)
        own_ref[target, :] = one[:rows]
        out_ref[target, 2 * third :] = one[rows:]
        out_ref[target, :third] = two[:rows]
        out_ref[target, third : 2 * third] = two[rows:]


def reduce_slots(send, keep, axis):
    bit = 1
    while True:
        got = exchange(send, axis, bit)
        total = keep.astype(F32) + got.astype(F32)
        if total.shape[0] == 1:
            return total[0]
        send = total[1::2].astype(BF16)
        keep = total[0::2].astype(BF16)
        bit *= 2


def spread_bits(size, swap=False):
    bits = []
    bit = size // 2
    while bit >= 1:
        bits.append(bit)
        bit //= 2
    if swap and len(bits) > 2:
        bits[0], bits[1] = bits[1], bits[0]
    return bits


def spread_place(s, bits):
    place = 0
    for bit in bits[:-1]:
        place = 2 * place + (1 if s & bit else 0)
    return place


def spread_slots(value, rows, axis, bits):
    width = value.shape[1]
    slots = 1
    while True:
        bit = bits[slots.bit_length() - 1]
        got = exchange(value, axis, bit)
        end = slots * rows
        rider = None
        if value.shape[0] > end:
            rider = value[end:].astype(F32) + got[end:].astype(F32)
        if bit == bits[-1]:
            return (value, got), rider
        pair = [v[:end].reshape(slots, rows, width) for v in (value, got)]
        value = jnp.stack(pair, axis=1).reshape(2 * end, width)
        if rider is not None:
            value = jnp.concatenate([value, rider.astype(BF16)], axis=0)
        slots *= 2


def reduce_rows(send, keep, mid, axis):
    rows = keep.shape[0]
    got = exchange(send, axis, 1).astype(F32)
    other = (mid + got[rows:]).astype(BF16)
    return keep + got[:rows] + exchange(other, axis, 2).astype(F32)


def body(
    tokens,
    gain_attention,
    gain_experts,
    proj_inputs,
    proj_output,
    bias_table,
    router_weight,
    routes,
    slot_index,
    drop_flags,
    expert_in,
    expert_out,
    cotangent,
):
    groups = lax.axis_size("wshard")
    size = lax.axis_size("expert")
    me = lax.axis_index("wshard")
    pos = lax.axis_index("expert")
    where = jnp.stack([me, pos]).astype(jnp.int32)
    count, width = tokens.shape
    length = count * groups
    heads_all = bias_table.shape[1]
    heads = heads_all // groups
    hs = width // heads_all
    part = width // groups
    local = expert_in.shape[0]
    experts = local * size
    hidden_local = expert_in.shape[2]
    buckets = bias_table.shape[0] * groups

    table = jnp.concatenate(
        [routes.T, slot_index.T, drop_flags.T, jnp.zeros((2, count), jnp.int32)], axis=0
    ).astype(F32)

    extra_rows = 16 + experts
    small = jnp.zeros((extra_rows, width), BF16)
    small = lax.dynamic_update_slice(small, bias_table.T, (0, me * bias_table.shape[0]))
    small = lax.dynamic_update_slice(
        small, jnp.stack([gain_attention, gain_experts]), (12, me * part)
    )
    small = lax.dynamic_update_slice(small, router_weight.T, (16, me * part))

    tok = gather_xor(tokens, "wshard")
    chunks = whole(
        lambda *r: prepare_kernel(groups, *r),
        [((3 * part // 2, 2 * part), BF16)] * groups,
        where,
        proj_inputs,
        scratch=[pltpu.VMEM((groups, 3 * part // 2, 2 * part), BF16)],
    )
    wp = [chunks[0]] + [exchange(chunks[k], "wshard", k) for k in range(1, groups)]
    ext = gather_xor(small, "wshard")
    wo = gather_xor(proj_output, "wshard")

    front = whole(
        lambda *r: front_kernel(groups, heads, hs, *r),
        [
            ((length, width), BF16),
            ((width, 3 * part), BF16),
            ((length, 3 * part), BF16),
            ((length, part), BF16),
            ((heads, length, length), F32),
        ]
        + [((count, part), BF16)] * groups,
        where,
        *tok,
        *wp,
        *ext,
        scratch=[pltpu.VMEM((extra_rows, width), F32)],
    )
    normed_one, wfull, projected, mixed, prob = front[:5]
    mine = front[5:]
    pieces = [mine[0]] + [exchange(mine[k], "wshard", k) for k in range(1, groups)]

    slots = experts * CAP
    residual, normed_two, send, gates = whole(
        lambda *r: middle_kernel(groups, experts, *r),
        [
            ((count, width), F32),
            ((count, width), BF16),
            ((slots, 2 * width), BF16),
            ((count, 128), F32),
        ],
        *pieces,
        *wo,
        *ext,
        tokens,
        cotangent,
        table,
        smem=0,
    )
    sent = lax.all_to_all(
        send.reshape(size, local * CAP, 2 * width), "expert", 0, 0, tiled=True
    ).reshape(slots, 2 * width)
    xs = gather_xor(sent, "wshard")

    rows = slots * groups
    fblock = 256
    steps = hidden_local // fblock
    full = pl.BlockSpec((slots, 2 * width), lambda f: (0, 0))
    hidden, gpre, back_send, back_keep, back_mid = pl.pallas_call(
        lambda *r: experts_kernel(groups, local, *r),
        grid=(steps,),
        in_specs=[full] * groups
        + [
            pl.BlockSpec((local, width, fblock), lambda f: (0, 0, f)),
            pl.BlockSpec((local, fblock, width), lambda f: (0, f, 0)),
        ],
        out_specs=[
            pl.BlockSpec((rows, fblock), lambda f: (0, f)),
            pl.BlockSpec((rows, fblock), lambda f: (0, f)),
            pl.BlockSpec((2 * slots, 2 * width), lambda f: (0, 0)),
            pl.BlockSpec((slots, 2 * width), lambda f: (0, 0)),
            pl.BlockSpec((slots, 2 * width), lambda f: (0, 0)),
        ],
        out_shape=[
            jax.ShapeDtypeStruct((rows, hidden_local), BF16),
            jax.ShapeDtypeStruct((rows, hidden_local), BF16),
            jax.ShapeDtypeStruct((2 * slots, 2 * width), BF16),
            jax.ShapeDtypeStruct((slots, 2 * width), F32),
            jax.ShapeDtypeStruct((slots, 2 * width), F32),
        ],
        scratch_shapes=[
            pltpu.VMEM((rows, 2 * width), BF16),
            pltpu.VMEM((rows, 2 * width), F32),
        ],
    )(*xs, expert_in, expert_out)

    full2 = pl.BlockSpec((slots, 2 * width), lambda j, f: (0, 0))
    weights_call = pl.pallas_call(
        lambda *r: weights_kernel(groups, local, *r),
        grid=(local, steps),
        in_specs=[full2] * groups
        + [
            pl.BlockSpec((rows, fblock), lambda j, f: (0, f)),
            pl.BlockSpec((rows, fblock), lambda j, f: (0, f)),
        ],
        out_specs=[
            pl.BlockSpec((1, width, fblock), lambda j, f: (j, 0, f)),
            pl.BlockSpec((1, fblock, width), lambda j, f: (j, f, 0)),
        ],
        out_shape=[
            jax.ShapeDtypeStruct(expert_in.shape, F32),
            jax.ShapeDtypeStruct(expert_out.shape, F32),
        ],
        scratch_shapes=[pltpu.VMEM((rows, 2 * width), BF16)],
    )
    grad_expert_in, grad_expert_out = weights_call(*xs, hidden, gpre)

    returned = reduce_rows(back_send, back_keep, back_mid, "wshard").astype(BF16)
    returned = lax.all_to_all(
        returned.reshape(size, local * CAP, 2 * width), "expert", 0, 0, tiled=True
    ).reshape(slots, 2 * width)

    output, grad_residual, grad_res_b, early = whole(
        lambda *r: return_kernel(groups, experts, *r),
        [
            ((count, width), BF16),
            ((count, width), F32),
            ((count, width), BF16),
            ((experts + 16, width), F32),
        ],
        *ext,
        returned,
        residual,
        normed_two,
        gates,
        cotangent,
        table,
        smem=0,
    )
    gr = gather_xor(grad_res_b, "wshard")
    fast = part % (8 * size) == 0
    cuts = size if fast else 0
    step = part // size
    first_shapes = [((part, width), BF16), ((width, part), BF16)]
    second_shapes = [((width, 2 * part), BF16), ((8, 128), BF16)]
    if fast:
        first_shapes = [((size // 2, 2 * step, width), BF16)] * 2
        second_shapes = [((size // 2, groups * step, 2 * part), BF16)] * 2
    gm, gv, first_send, first_keep = whole(
        lambda *r: values_kernel(groups, heads, hs, cuts, *r),
        [((length, part), BF16), ((length, part), BF16)] + first_shapes,
        where,
        *gr,
        proj_output,
        mixed,
        prob,
        normed_one,
        scratch=[
            pltpu.VMEM((length, width), BF16),
            pltpu.VMEM((part, width), F32),
            pltpu.VMEM((width, part), F32),
        ],
    )
    second_send, second_keep, gproj, tiles = whole(
        lambda *r: scores_kernel(groups, heads, hs, cuts, *r),
        second_shapes
        + [((length, 3 * part), BF16), ((heads, BLOCK, 3 * BLOCK), F32)],
        where,
        gm,
        gv,
        projected,
        prob,
        normed_one,
        scratch=[pltpu.VMEM((width, 2 * part), F32)],
    )
    gn_send, gn_keep, gn_mid, sums = whole(
        lambda *r: rest_kernel(groups, heads, *r),
        [
            ((2 * count + experts + 16, width), BF16),
            ((count, width), F32),
            ((count, width), F32),
            ((experts + 16, width), F32),
        ],
        where,
        *tok,
        gproj,
        wfull,
        tiles,
        early,
        scratch=[pltpu.VMEM((length, width), F32)],
    )
    got = exchange(gn_send, "wshard", 1).astype(F32)
    sums = sums + got[2 * count :]
    other = jnp.concatenate([gn_mid + got[count : 2 * count], sums], axis=0).astype(BF16)
    other = exchange(other, "wshard", 2).astype(F32)
    grad_normed_one = gn_keep + got[:count] + other[:count]
    sums = sums + other[count:]
    inputs = tokens.astype(F32)
    scale_one = norm_scale(inputs)
    gain_one_f = sum(e[12:13].astype(F32) for e in ext)
    scaled = grad_normed_one * gain_one_f
    inner = jnp.mean(scaled * inputs, axis=-1, keepdims=True)
    grad_tokens = grad_residual + (
        scale_one * scaled - inputs * scale_one * scale_one * scale_one * inner
    )

    lines = experts + 16
    sums = lax.dynamic_slice(sums, (0, me * part), (lines, part))

    if fast:
        one = reduce_slots(first_send, first_keep, "expert").astype(BF16)
        two = reduce_slots(second_send, second_keep, "expert").astype(BF16)
        cut = [
            jnp.concatenate(
                [two[t * step : (t + 1) * step], one[step:, t * part : (t + 1) * part]], axis=1
            )
            for t in range(groups)
        ]
        cut = [cut[0]] + [exchange(cut[t], "wshard", t) for t in range(1, groups)]
        one, two = whole(
            lambda *r: join_kernel(groups, *r),
            [((2 * step + lines // groups, width), BF16), ((2 * step, width), BF16)],
            where,
            *cut,
            one[:step],
            sums.reshape(lines // groups, width),
        )
        one, sums = spread_slots(one, 2 * step, "expert", spread_bits(size))
        sums = sums.reshape(lines, part)
        two, _ = spread_slots(two, 2 * step, "expert", spread_bits(size, True))
        total_inputs, total_output = whole(
            lambda *r: final_kernel(size, *r),
            [((part, 3 * width), F32), ((part, width), F32)],
            where,
            *one,
            *two,
        )
    else:
        sums = lax.psum(sums, "expert")
        total_output = lax.psum(first_send.astype(F32), "expert")
        total = jnp.concatenate([second_send, first_keep], axis=1)
        total = lax.psum(total, "expert").reshape(groups, part, 3, part)
        total = lax.all_to_all(total, "wshard", 0, 0, tiled=True)
        total_inputs = total.transpose(1, 2, 0, 3).reshape(part, 3 * width).astype(F32)
    grad_router = sums[16:].T
    grad_gain_two = sums[13]
    grad_gain_one = sums[12]
    grad_table = sums[:heads_all, : buckets // groups].T
    return (
        output,
        grad_tokens,
        grad_gain_one,
        grad_gain_two,
        total_inputs,
        total_output,
        grad_table,
        grad_router,
        grad_expert_in,
        grad_expert_out,
    )


def solution(mesh):
    placed = (
        P(("expert", "wshard"), None),
        P("wshard"),
        P("wshard"),
        P("wshard", None),
        P("wshard", None),
        P("wshard", None),
        P("wshard", None),
        P(("expert", "wshard"), None),
        P(("expert", "wshard"), None),
        P(("expert", "wshard"), None),
        P("expert", None, "wshard"),
        P("expert", "wshard", None),
        P(("expert", "wshard"), None),
    )
    return jax.shard_map(
        body,
        mesh=mesh,
        in_specs=placed,
        out_specs=(
            P(("expert", "wshard"), None),
            P(("expert", "wshard"), None),
            P("wshard"),
            P("wshard"),
            P("wshard", None),
            P("wshard", None),
            P("wshard", None),
            P("wshard", None),
            P("expert", None, "wshard"),
            P("expert", "wshard", None),
        ),
        check_vma=False,
    )
```
